512 devices in a mesh: grp: 8 (over z), ep: 64 (over y, x, core).
Axes of the slice: x: 4, y: 8, z: 8, core: 2. Of those that a mesh axis runs over, the one named last changes fastest.
Arguments:
- tokens: bfloat16 [65536, 512], P(('grp', 'ep')), may hold values from -6 to 6
- teacher: bfloat16 [65536, 7168], P(('grp', 'ep')), may hold values from -6 to 6
- expert_ids: int32 [65536, 4], P(('grp', 'ep')), may hold values from 0 to 63, all different within a row; in each aligned block of 128 rows (0 to 127, 128 to 255, ...) at most 12 rows name the same one
- route_weights: float32 [65536, 4], P(('grp', 'ep')), may hold values from 0.1 to 1
- w_gate: bfloat16 [64, 512, 1024], P('ep', 'grp'), may hold values from -0.25 to 0.25
- w_up: bfloat16 [64, 512, 1024], P('ep', 'grp'), may hold values from -0.25 to 0.25
- w_down: bfloat16 [64, 1024, 512], P('ep', 'grp'), may hold values from -0.1875 to 0.1875
- critic_teacher: bfloat16 [7168, 512], P('ep'), may hold values from -0.0625 to 0.0625
- critic_student: bfloat16 [512, 512], P('ep'), may hold values from -0.25 to 0.25
- critic_head: float32 [512], replicated, may hold values from -0.25 to 0.25
Outputs:
- grad_gate: float32 [64, 512, 1024], P('ep', 'grp')
- grad_up: float32 [64, 512, 1024], P('ep', 'grp')
- grad_down: float32 [64, 1024, 512], P('ep', 'grp')
- scores: float32 [65536], P(('grp', 'ep'))
The draws below stay inside these ranges and needn't reach their ends.
Inputs may be any that keep to these rules, and one draw needn't show every extreme that they name: `expert_ids`: each row names 4 different experts. Among the 128 rows of one device no expert is named more than 12 times, and in every draw some expert is named exactly 12 times by the rows of some device.
All inputs are finite; a program needn't handle non-finite values.
Results may differ from the reference program's by a relative error of at most 0.013.
Values may be sent and summed in bfloat16 or wider, within the bound.
No kernel may reach another device: no remote copies, remote signals or barrier semaphores. Data moves between devices by JAX's collectives and lax.ppermute only.
A program may use at most 64 MiB of HBM per device.

```python
import math
import jax
import jax.numpy as jnp
import numpy as np
from jax import lax

D = 512
H = 1024
DT = 7168
K = 512
TOP = 4
TOK_DEV = 128
EXPERTS = 64
CAP = 12
TOKENS = 65536
N_GRP = 8
N_EP = 64


def block_scale(key, extent, cuts, smallest, largest):
    def one(axis_at, shards_of):
        draws = jax.random.uniform(jax.random.fold_in(jax.random.fold_in(key, 6), axis_at), (shards_of,), jnp.float32, smallest / len(cuts), largest / len(cuts))
        return jnp.repeat(jnp.exp(draws), extent[axis_at] // shards_of).reshape((-1,) + (1,) * (len(extent) - axis_at - 1))

    level = one(*cuts[0])
    for cut in cuts[1:]:
        level = level * one(*cut)
    return level


def deal_out(stream_key, own, number, rows, number_of, top, most, lean):
    sequence = jax.random.permutation(stream_key, number_of)
    heavy_load, common = shares(number_of, rows * top, most, lean, True), shares(number_of, rows * top, most, lean, False)
    places = jnp.arange(number_of)

    def named(lengths, turn):
        used = int((lengths > 0).sum())
        fixed = max(1, used // 4)
        passed = fixed + (places - fixed + turn * (used - fixed)) % max(1, number_of - fixed)
        return jnp.zeros((number_of,), jnp.int32).at[sequence[jnp.where(places < fixed, places, passed)]].set(jnp.asarray(lengths, jnp.int32))

    lengths = jnp.where(number % 4 == 0, named(heavy_load, number // 4), named(common, number - number // 4 - 1))
    mixed = jax.random.permutation(jax.random.fold_in(own, 3), number_of)
    source_of, receiver = mixed[0:number_of // 2 * 2:2], mixed[1:number_of // 2 * 2:2]
    room = jnp.minimum(lengths[source_of] - 1, most - lengths[receiver]) // 2
    room = jnp.where((source_of == sequence[0]) | (receiver == sequence[0]) | (lengths[receiver] == 0), 0, jnp.maximum(room, 0))
    passed = jax.random.randint(jax.random.fold_in(own, 4), (number_of // 2,), 0, 1 << 20) % (room + 1)
    lengths = lengths.at[source_of].add(-passed).at[receiver].add(passed)
    items = jnp.searchsorted(jnp.cumsum(lengths), jnp.arange(rows * top), side="right").astype(jnp.int32)
    table = items.reshape(top, rows).T
    table = table[jax.random.permutation(jax.random.fold_in(own, 1), rows)]
    turn = jax.random.randint(jax.random.fold_in(own, 2), (rows, 1), 0, top)
    return jnp.take_along_axis(table, (jnp.arange(top)[None, :] + turn) % top, axis=1)


def shares(amount, total, reach, skew, full):
    loads = [(1 << 20) // math.isqrt(rank ** skew) + 1 for rank in range(1, amount + 1)]
    largest = reach if full else min(reach, max(-(-total // amount), total * loads[0] // sum(loads)))
    least = 1 if total - largest >= amount - 1 else 0
    counts, surplus = [largest] + [least] * (amount - 1), total - largest - least * (amount - 1)
    while surplus > 0:
        free = [i for i in range(1, amount) if counts[i] < largest] or [i for i in range(1, amount) if counts[i] < reach]
        whole, left = sum([loads[i] for i in free]), surplus
        for i in free:
            extra = min(reach - counts[i], max(1, left * loads[i] // whole), surplus)
            counts[i] = counts[i] + extra
            surplus = surplus - extra
    return np.array(counts)


def scatter_about(rng, dims, scale, limit, shards=(), kind=jnp.bfloat16):
    entries = jax.random.normal(rng, dims, jnp.float32) * scale
    if len(shards) > 0:
        entries = block_scale(rng, dims, shards, -0.22, 0.18) * entries
    return jnp.clip(entries, min=-limit, max=limit).astype(kind)


def setup_inputs(seed: int = 0) -> dict:
    splits = jax.random.split(jax.random.key(seed), 11)
    tokens = scatter_about(splits[0], (TOKENS, D), 1.0, 6.0, ((0, 512),))
    teacher = scatter_about(splits[1], (TOKENS, DT), 1.0, 6.0, ((0, 512),))
    expert_ids_keys = jax.random.split(jax.random.fold_in(splits[2], 1), TOKENS // TOK_DEV)
    expert_ids_turns = jax.random.permutation(jax.random.fold_in(splits[2], 3), TOKENS // TOK_DEV)
    expert_ids = jax.vmap(lambda own, number: deal_out(jax.random.fold_in(splits[2], 2), own, number, TOK_DEV, EXPERTS, TOP, CAP, 2))(expert_ids_keys, expert_ids_turns).reshape((TOKENS, TOP))
    route_weights = jnp.clip(jnp.exp(math.log(1.0) - 2.3025851 * jax.random.uniform(splits[3], (TOKENS, TOP), jnp.float32) ** block_scale(splits[3], (TOKENS, TOP), ((0, 512),), -0.2, 0.2)), 0.1, 1.0)
    w_gate = scatter_about(splits[4], (EXPERTS, D, H), D ** -0.5, 0.25, ((0, 64), (1, 8)))
    w_up = scatter_about(splits[5], (EXPERTS, D, H), D ** -0.5, 0.25, ((0, 64), (1, 8)))
    w_down = scatter_about(splits[6], (EXPERTS, H, D), H ** -0.5, 0.1875, ((0, 64), (1, 8)))
    critic_teacher = scatter_about(splits[7], (DT, K), DT ** -0.5, 0.0625, ((0, 64),))
    critic_student = scatter_about(splits[8], (D, K), D ** -0.5, 0.25, ((0, 64),))
    critic_head = scatter_about(splits[9], (K,), K ** -0.5, 0.25, (), jnp.float32)
    return {"tokens": tokens, "teacher": teacher, "expert_ids": expert_ids, "route_weights": route_weights, "w_gate": w_gate, "w_up": w_up, "w_down": w_down, "critic_teacher": critic_teacher, "critic_student": critic_student, "critic_head": critic_head}


def gelu_tanh(value):
    inner = 0.7978845608 * (value + 0.044715 * value * value * value)
    return 0.5 * value * (1.0 + jnp.tanh(inner))


def gelu_slope(value):
    inner = 0.7978845608 * (value + 0.044715 * value * value * value)
    tangent = jnp.tanh(inner)
    return 0.5 * (1.0 + tangent) + 0.5 * value * (1.0 - tangent * tangent) * 0.7978845608 * (1.0 + 3.0 * 0.044715 * value * value)


def slots_of(ids):
    flat = ids.reshape(-1).astype(jnp.int32)
    onehot = (flat[:, None] == jnp.arange(EXPERTS, dtype=jnp.int32)[None, :]).astype(jnp.int32)
    before = jnp.cumsum(onehot, axis=0) - onehot
    return (flat * CAP + jnp.sum(before * onehot, axis=1)).astype(jnp.int32)


def place(slots, rows):
    return jnp.zeros((EXPERTS * CAP, rows.shape[-1]), rows.dtype).at[slots].set(rows)


def to_experts(buffer):
    return buffer.reshape(N_EP, EXPERTS, CAP, D).transpose(1, 0, 2, 3).reshape(EXPERTS, N_EP * CAP, D)


def from_experts(buffer):
    return buffer.reshape(EXPERTS, N_EP, CAP, D).transpose(1, 0, 2, 3).reshape(N_EP, EXPERTS * CAP, D)


def rounded(value):
    low = lax.optimization_barrier(value.astype(jnp.bfloat16))
    return low.astype(jnp.float32)


def reference(tokens, teacher, expert_ids, route_weights, w_gate, w_up, w_down, critic_teacher, critic_student, critic_head):
    rows = N_EP * TOK_DEV
    wg32 = w_gate.astype(jnp.float32)
    wu32 = w_up.astype(jnp.float32)
    wd32 = w_down.astype(jnp.float32)
    items = (tokens.reshape(N_GRP, N_EP, TOK_DEV, D),
             teacher.reshape(N_GRP, rows, DT),
             expert_ids.reshape(N_GRP, N_EP, TOK_DEV * TOP),
             route_weights.reshape(N_GRP, N_EP, TOK_DEV, TOP))

    def group_step(carry, item):
        acc_gate, acc_up, acc_down = carry
        xs, feats, ids, weights = item
        slots = jax.vmap(slots_of)(ids)
        spread = jnp.repeat(xs, TOP, axis=1)
        routed = to_experts(jax.vmap(place)(slots, spread))
        routed32 = routed.astype(jnp.float32)
        gate = jnp.einsum("erd,edh->erh", routed32, wg32)
        up = jnp.einsum("erd,edh->erh", routed32, wu32)
        hidden = (jax.nn.silu(gate) * up).astype(jnp.bfloat16)
        hidden32 = hidden.astype(jnp.float32)
        expert_out = jnp.einsum("erh,ehd->erd", hidden32, wd32).astype(jnp.bfloat16)
        back = from_experts(expert_out)
        picked = jax.vmap(lambda buf, sl: buf[sl])(back, slots).reshape(N_EP, TOK_DEV, TOP, D)
        student = jnp.sum(picked.astype(jnp.float32) * weights[..., None], axis=2).astype(jnp.bfloat16)
        student = student.reshape(rows, D)
        pre = jnp.dot(feats, critic_teacher, preferred_element_type=jnp.float32) + jnp.dot(student, critic_student, preferred_element_type=jnp.float32)
        score = jnp.sum(gelu_tanh(pre) * critic_head[None, :], axis=1)
        dscore = -jax.nn.sigmoid(-score)
        dpre = (dscore[:, None] * critic_head[None, :] * gelu_slope(pre)).astype(jnp.bfloat16)
        dstudent = jnp.dot(dpre, critic_student.T, preferred_element_type=jnp.float32).reshape(N_EP, TOK_DEV, 1, D)
        dassign = (weights[..., None] * dstudent).astype(jnp.bfloat16).reshape(N_EP, TOK_DEV * TOP, D)
        droute = to_experts(jax.vmap(place)(slots, dassign)).astype(jnp.float32)
        dhidden = jnp.einsum("erd,ehd->erh", droute, wd32)
        sig = jax.nn.sigmoid(gate)
        dgate = (dhidden * up * sig * (1.0 + gate * (1.0 - sig))).astype(jnp.bfloat16).astype(jnp.float32)
        dup = (dhidden * gate * sig).astype(jnp.bfloat16).astype(jnp.float32)
        part_gate = jnp.einsum("erd,erh->edh", routed32, dgate)
        part_up = jnp.einsum("erd,erh->edh", routed32, dup)
        part_down = jnp.einsum("erh,erd->ehd", hidden32, droute)
        carry = (acc_gate + rounded(part_gate), acc_up + rounded(part_up), acc_down + rounded(part_down))
        return carry, score

    start = (jnp.zeros((EXPERTS, D, H), jnp.float32), jnp.zeros((EXPERTS, D, H), jnp.float32), jnp.zeros((EXPERTS, H, D), jnp.float32))
    sums, scores = lax.scan(group_step, start, items)
    return sums[0], sums[1], sums[2], scores.reshape(TOKENS)
```

```python
import jax
import jax.numpy as jnp
from jax import lax
from jax.sharding import Mesh
from jax.sharding import PartitionSpec as P

TOP = 4
EP = ("yx", "c")
BF = jnp.bfloat16
F32 = jnp.float32


def gelu_tanh(value):
    inner = 0.7978845608 * (value + 0.044715 * value * value * value)
    return 0.5 * value * (1.0 + jnp.tanh(inner))


def gelu_slope(value):
    inner = 0.7978845608 * (value + 0.044715 * value * value * value)
    tangent = jnp.tanh(inner)
    return 0.5 * (1.0 + tangent) + 0.5 * value * (1.0 - tangent * tangent) * 0.7978845608 * (
        1.0 + 3.0 * 0.044715 * value * value
    )


def dot(left, right, dims=((1,), (0,))):
    return lax.dot_general(left, right, (dims, ((), ())), preferred_element_type=F32)


def split(value):
    high = value.astype(BF)
    return high, (value - high.astype(F32)).astype(BF)


def shift(value, axis, step):
    count = lax.axis_size(axis)
    return lax.ppermute(value, axis, [(i, (i + step) % count) for i in range(count)])


def swap(value):
    return shift(value, "c", 1)


def both(core, own, other):
    first = core == 0
    return jnp.stack([jnp.where(first, own, other), jnp.where(first, other, own)])


def ring_gather(block):
    count = lax.axis_size("grp")
    here = lax.axis_index("grp")
    full = jnp.zeros((count,) + block.shape, block.dtype)

    def put(full, piece, at):
        return lax.dynamic_update_slice(full, piece[None], (at % count, 0, 0))

    full = put(full, block, here)
    up = down = block
    for step in range(1, count // 2 + 1):
        up = shift(up, "grp", 1)
        full = put(full, up, here - step + count)
        if 2 * step < count:
            down = shift(down, "grp", -1)
            full = put(full, down, here + step)
    return full


def body(
    tokens,
    teacher,
    expert_ids,
    route_weights,
    w_gate,
    w_up,
    w_down,
    critic_teacher,
    critic_student,
    critic_head,
):
    core = lax.axis_index("c")
    chips = lax.axis_size("yx")
    experts = 2 * chips
    tok_dev, width = tokens.shape
    capacity = 3 * tok_dev * TOP // (2 * experts)
    slots = experts * capacity
    hidden_all = w_gate.shape[2]
    half = hidden_all // 2
    rows_in = w_gate.shape[1]

    teacher_rows = lax.all_gather(critic_teacher, EP, axis=0, tiled=True)
    pack = jnp.concatenate(
        [w_gate[0, :, :half], w_gate[0, :, half:], w_up[0, :, :half], w_up[0, :, half:], w_down[0]]
    )
    full = ring_gather(pack)

    meta = jnp.concatenate([expert_ids.T.astype(F32), route_weights.T])
    tok2 = both(core, tokens, swap(tokens)).reshape(2 * tok_dev, width)
    meta2 = both(core, meta, swap(meta))
    ids = meta2[:, :TOP].astype(jnp.int32)
    weights = meta2[:, TOP:]
    member = ids[:, :, None, :] == jnp.arange(experts, dtype=jnp.int32)[None, None, :, None]
    count = jnp.sum(member.astype(F32), axis=1).astype(BF)
    order = jnp.arange(tok_dev)
    earlier = (order[:, None] < order[None, :]).astype(BF)
    before = lax.dot_general(count, earlier, (((2,), (0,)), ((), ())), preferred_element_type=F32)
    rank = jnp.sum(jnp.where(member, before[:, None], 0.0), axis=2).astype(jnp.int32)
    source = jnp.arange(2, dtype=jnp.int32)[:, None, None]
    place = (ids // 2) * (2 * capacity) + source * capacity + rank
    place = jnp.where(ids % 2 == core, place, -1)
    place = place.transpose(1, 0, 2).reshape(TOP, 2 * tok_dev)
    weights = weights.transpose(1, 0, 2).reshape(TOP, 2 * tok_dev)
    hits = place[:, None, :] == jnp.arange(slots, dtype=jnp.int32)[None, :, None]
    pick = jnp.sum(hits.astype(F32), axis=0).astype(BF)
    scaled = jnp.sum(jnp.where(hits, weights[:, None, :], 0.0), axis=0)
    row_weight = jnp.sum(scaled, axis=1)
    scaled_high, scaled_low = split(scaled)

    outbound = dot(pick, tok2).astype(BF).reshape(chips, 2 * capacity, width)
    rows_st = critic_student.shape[0]
    outbound = jnp.concatenate(
        [outbound, jnp.broadcast_to(critic_student[None], (chips, rows_st, width))], axis=1
    )
    inbound = lax.all_to_all(outbound, "yx", split_axis=0, concat_axis=0, tiled=True)
    routed = inbound[:, : 2 * capacity].reshape(slots, width)
    student_half = inbound[:, 2 * capacity :]
    student_rows = (
        both(core, student_half, swap(student_half)).transpose(1, 0, 2, 3).reshape(width, -1)
    )

    gate_w = jnp.concatenate(
        [full[:, :rows_in].reshape(width, half), full[:, rows_in : 2 * rows_in].reshape(width, half)],
        axis=1,
    )
    up_w = jnp.concatenate(
        [
            full[:, 2 * rows_in : 3 * rows_in].reshape(width, half),
            full[:, 3 * rows_in : 4 * rows_in].reshape(width, half),
        ],
        axis=1,
    )
    down_w = full[:, 4 * rows_in :].reshape(hidden_all, width)
    gate = dot(routed, gate_w)
    up = dot(routed, up_w)
    sig = jax.nn.sigmoid(gate)
    hidden = (gate * sig * up).astype(BF)
    expert_out = dot(hidden, down_w).astype(BF)
    returned = lax.all_to_all(
        expert_out.reshape(chips, 2 * capacity, width), "yx", split_axis=0, concat_axis=0, tiled=True
    ).reshape(slots, width)

    partial = dot(scaled_high, returned, ((0,), (0,))) + dot(scaled_low, returned, ((0,), (0,)))
    partial = partial.reshape(2, tok_dev, width)
    mine = lax.dynamic_index_in_dim(partial, core, 0, keepdims=False)
    theirs = lax.dynamic_index_in_dim(partial, 1 - core, 0, keepdims=False)
    student = (mine + swap(theirs)).astype(BF)
    pre = dot(teacher, teacher_rows) + dot(student, student_rows)
    score = jnp.sum(gelu_tanh(pre) * critic_head[None, :], axis=1)
    dscore = -jax.nn.sigmoid(-score)
    dpre = (dscore[:, None] * critic_head[None, :] * gelu_slope(pre)).astype(BF)
    dpre2 = both(core, dpre, swap(dpre)).reshape(2 * tok_dev, -1)
    dstudent = dot(dpre2, student_rows, ((1,), (1,)))
    ds_high, ds_low = split(dstudent)
    grad_rows = dot(pick, ds_high) + dot(pick, ds_low)
    grad_out = (grad_rows * row_weight[:, None]).astype(BF)
    droute = lax.all_to_all(
        grad_out.reshape(chips, 2 * capacity, width), "yx", split_axis=0, concat_axis=0, tiled=True
    ).reshape(slots, width)

    dhidden = dot(droute, down_w, ((1,), (1,)))
    part_down = dot(hidden, droute, ((0,), (0,))).astype(BF)
    dgate = (dhidden * up * sig * (1.0 + gate * (1.0 - sig))).astype(BF)
    dup = (dhidden * gate * sig).astype(BF)
    part_gate = dot(routed, dgate, ((0,), (0,))).astype(BF)
    part_up = dot(routed, dup, ((0,), (0,))).astype(BF)
    groups = lax.axis_size("grp")

    def by_group(value):
        return value.reshape(groups, -1, width)

    parts = jnp.concatenate(
        [
            by_group(part_gate[:, :half]),
            by_group(part_gate[:, half:]),
            by_group(part_up[:, :half]),
            by_group(part_up[:, half:]),
            by_group(part_down),
        ],
        axis=1,
    )
    total = lax.psum_scatter(
        parts.reshape(-1, width), "grp", scatter_dimension=0, tiled=True
    ).astype(F32)
    grad_gate = jnp.concatenate([total[:rows_in], total[rows_in : 2 * rows_in]], axis=1)[None]
    grad_up = jnp.concatenate(
        [total[2 * rows_in : 3 * rows_in], total[3 * rows_in : 4 * rows_in]], axis=1
    )[None]
    return (grad_gate, grad_up, total[4 * rows_in :][None], score)


def solution(mesh):
    groups, members = mesh.devices.shape
    fine = Mesh(mesh.devices.reshape(groups, members // 2, 2), ("grp",) + EP)
    rows = P(("grp",) + EP, None)
    weights = P(EP, "grp", None)
    critic = P(EP, None)
    in_specs = (rows, rows, rows, rows, weights, weights, weights, critic, critic, P())
    out_specs = (weights, weights, weights, P(("grp",) + EP))
    return jax.shard_map(body, mesh=fine, in_specs=in_specs, out_specs=out_specs, check_vma=False)
```

```python
import functools

import jax
import jax.numpy as jnp
from jax import lax
from jax.experimental import pallas as pl
from jax.experimental.pallas import tpu as pltpu
from jax.sharding import Mesh
from jax.sharding import PartitionSpec as P

TOP = 4
EP = ("yx", "c")
BF = jnp.bfloat16
F32 = jnp.float32


def gelu_tanh(value):
    inner = 0.7978845608 * (value + 0.044715 * value * value * value)
    return 0.5 * value * (1.0 + jnp.tanh(inner))


def gelu_slope(value):
    inner = 0.7978845608 * (value + 0.044715 * value * value * value)
    tangent = jnp.tanh(inner)
    return 0.5 * (1.0 + tangent) + 0.5 * value * (1.0 - tangent * tangent) * 0.7978845608 * (
        1.0 + 3.0 * 0.044715 * value * value
    )


def dot(left, right, dims=((1,), (0,))):
    return lax.dot_general(left, right, (dims, ((), ())), preferred_element_type=F32)


def split(value):
    high = value.astype(BF)
    return high, (value - high.astype(F32)).astype(BF)


def shift(value, axis, step):
    count = lax.axis_size(axis)
    return lax.ppermute(value, axis, [(i, (i + step) % count) for i in range(count)])


def swap(value):
    return shift(value, "c", 1)


def both(core, own, other):
    first = core == 0
    return jnp.stack([jnp.where(first, own, other), jnp.where(first, other, own)])


def ring_gather(block):
    count = lax.axis_size("grp")
    pieces = [block] + [None] * (count - 1)
    up = down = block
    for step in range(1, count // 2 + 1):
        up = shift(up, "grp", 1)
        pieces[step] = up
        if 2 * step < count:
            down = shift(down, "grp", -1)
            pieces[count - step] = down
    return pieces


VMEM = pl.BlockSpec(memory_space=pltpu.VMEM)
SMEM = pl.BlockSpec(memory_space=pltpu.SMEM)
ANY = pl.BlockSpec(memory_space=pl.ANY)


def pack_kernel(gate_ref, up_ref, down_ref, out_ref):
    rows, hidden = gate_ref.shape
    half = hidden // 2
    out_ref[0:rows] = gate_ref[:, :half]
    out_ref[rows : 2 * rows] = gate_ref[:, half:]
    out_ref[2 * rows : 3 * rows] = up_ref[:, :half]
    out_ref[3 * rows : 4 * rows] = up_ref[:, half:]
    out_ref[4 * rows :] = down_ref[...]


def pack_weights(gate, up, down):
    rows = 4 * gate.shape[0] + down.shape[0]
    return pl.pallas_call(
        pack_kernel,
        out_shape=jax.ShapeDtypeStruct((rows, down.shape[1]), BF),
        in_specs=[VMEM] * 3,
        out_specs=VMEM,
        name="pack",
    )(gate, up, down)


def unpack_kernel(in_ref, gate_ref, up_ref, down_ref):
    rows, hidden = gate_ref.shape
    half = hidden // 2
    gate_ref[:, :half] = in_ref[0:rows].astype(F32)
    gate_ref[:, half:] = in_ref[rows : 2 * rows].astype(F32)
    up_ref[:, :half] = in_ref[2 * rows : 3 * rows].astype(F32)
    up_ref[:, half:] = in_ref[3 * rows : 4 * rows].astype(F32)
    down_ref[...] = in_ref[4 * rows :].astype(F32)


def unpack_grads(total, rows, half):
    return pl.pallas_call(
        unpack_kernel,
        out_shape=[
            jax.ShapeDtypeStruct((rows, 2 * half), F32),
            jax.ShapeDtypeStruct((rows, 2 * half), F32),
            jax.ShapeDtypeStruct((total.shape[0] - 4 * rows, total.shape[1]), F32),
        ],
        in_specs=[VMEM],
        out_specs=[VMEM] * 3,
        name="unpack",
    )(total)


def fetch(count, here_ref, pieces, target, sems, first):
    copies = []
    for k in range(count):
        at = lax.rem(here_ref[0] - k + count, count)
        piece = pieces[k].at[pl.ds(first, target.shape[1])]
        copies.append(pltpu.make_async_copy(piece, target.at[at], sems.at[k]))
    return copies


def forward_kernel(count, rows, here_ref, routed_ref, *refs):
    pieces = refs[:count]
    hid_ref, coef_gate_ref, coef_up_ref, out_ref, full, sems = refs[count:]

    @pl.when(pl.program_id(0) == 0)
    def _():
        copies = fetch(count, here_ref, pieces, full, sems, 0)
        for copy in copies:
            copy.start()
        for copy in copies:
            copy.wait()

    width = routed_ref.shape[1]
    half = full.shape[2]
    routed = routed_ref[...]
    out = jnp.zeros(out_ref.shape, F32)
    for part in range(2):
        gate_w = full[:, part * rows : (part + 1) * rows].reshape(width, half)
        up_w = full[:, (2 + part) * rows : (3 + part) * rows].reshape(width, half)
        gate = jnp.dot(routed, gate_w, preferred_element_type=F32)
        up = jnp.dot(routed, up_w, preferred_element_type=F32)
        sig = jax.nn.sigmoid(gate)
        silu = gate * sig
        hid = (silu * up).astype(BF)
        span = slice(part * half, (part + 1) * half)
        hid_ref[:, span] = hid
        coef_up_ref[:, span] = silu.astype(BF)
        coef_gate_ref[:, span] = (up * (sig + silu * (1.0 - sig))).astype(BF)
        group = count // 2
        down_w = full[part * group : (part + 1) * group, 4 * rows :].reshape(half, width)
        out += jnp.dot(hid, down_w, preferred_element_type=F32)
    out_ref[...] = out.astype(BF)


def expert_forward(here, routed, pieces, rows, tile=384):
    count = len(pieces)
    slots, width = routed.shape
    half = pieces[0].shape[1]
    hidden = 2 * half
    block = lambda cols: pl.BlockSpec((tile, cols), lambda i: (i, 0))
    wide = jax.ShapeDtypeStruct((slots, hidden), BF)
    return pl.pallas_call(
        functools.partial(forward_kernel, count, rows),
        grid=(slots // tile,),
        out_shape=[wide, wide, wide, jax.ShapeDtypeStruct((slots, width), BF)],
        in_specs=[SMEM, block(width)] + [ANY] * count,
        out_specs=[block(hidden), block(hidden), block(hidden), block(width)],
        scratch_shapes=[
            pltpu.VMEM((count,) + pieces[0].shape, BF),
            pltpu.SemaphoreType.DMA((count,)),
        ],
        cost_estimate=pl.CostEstimate(
            flops=6 * slots * width * hidden,
            transcendentals=slots * hidden,
            bytes_accessed=6 * slots * hidden + 6 * width * hidden,
        ),
        name="expert_forward",
    )(here, routed, *pieces)


def backward_kernel(count, rows, here_ref, droute_ref, routed_ref, hid_ref, cg_ref, cu_ref, *refs):
    pieces = refs[:count]
    out_ref, down, parts, sems, out_sems = refs[count:]
    step = pl.program_id(0)
    width, half = routed_ref.shape[1], hid_ref.shape[1]
    each = down.shape[1]
    take = count // 2

    @pl.when(step == 0)
    def _():
        copies = fetch(count, here_ref, pieces, down, sems, 4 * rows)
        for copy in copies:
            copy.start()
        for copy in copies:
            copy.wait()

    droute = droute_ref[...]
    routed = routed_ref[...]
    down_w = down[pl.ds(step * take, take)].reshape(half, width)
    dhid = lax.dot_general(droute, down_w, (((1,), (1,)), ((), ())), preferred_element_type=F32)
    dgate = (dhid * cg_ref[...].astype(F32)).astype(BF)
    dup = (dhid * cu_ref[...].astype(F32)).astype(BF)
    rows_dot = functools.partial(
        lax.dot_general, dimension_numbers=(((0,), (0,)), ((), ())), preferred_element_type=F32
    )
    part_down = rows_dot(hid_ref[...], droute).astype(BF).reshape(take, each, width)
    part_gate = rows_dot(routed, dgate).astype(BF).reshape(count, rows, half)
    part_up = rows_dot(routed, dup).astype(BF).reshape(count, rows, half)

    def leaving(at):
        places = [(pl.ds(at * take, take), pl.ds(4 * rows, each))]
        places += [(slice(None), pl.ds(block * rows, rows)) for block in (at, 2 + at)]
        return [
            pltpu.make_async_copy(parts.at[place], out_ref.at[place], out_sems.at[3 * at + k])
            for k, place in enumerate(places)
        ]

    for at in range(2):

        @pl.when(step == at)
        def _():
            parts[at * take : (at + 1) * take, 4 * rows :] = part_down
            parts[:, at * rows : (at + 1) * rows] = part_gate
            parts[:, (2 + at) * rows : (3 + at) * rows] = part_up
            for copy in leaving(at):
                copy.start()

    @pl.when(step == 1)
    def _():
        for at in range(2):
            for copy in leaving(at):
                copy.wait()


def expert_backward(here, droute, routed, hid, coef_gate, coef_up, pieces, rows):
    count = len(pieces)
    slots, width = routed.shape
    hidden = hid.shape[1]
    whole = pl.BlockSpec((slots, width), lambda i: (0, 0))
    block = pl.BlockSpec((slots, hidden // 2), lambda i: (0, i))
    shape = (count,) + pieces[0].shape
    return pl.pallas_call(
        functools.partial(backward_kernel, count, rows),
        grid=(2,),
        out_shape=jax.ShapeDtypeStruct(shape, BF),
        in_specs=[SMEM, whole, whole, block, block, block] + [ANY] * count,
        out_specs=ANY,
        scratch_shapes=[
            pltpu.VMEM((count, shape[1] - 4 * rows, width), BF),
            pltpu.VMEM(shape, BF),
            pltpu.SemaphoreType.DMA((count,)),
            pltpu.SemaphoreType.DMA((6,)),
        ],
        cost_estimate=pl.CostEstimate(
            flops=8 * slots * width * hidden,
            transcendentals=0,
            bytes_accessed=6 * slots * hidden + 6 * width * hidden,
        ),
        name="expert_backward",
    )(here, droute, routed, hid, coef_gate, coef_up, *pieces)


def layer(
    tokens,
    teacher,
    expert_ids,
    route_weights,
    w_gate,
    w_up,
    w_down,
    critic_teacher,
    critic_student,
    critic_head,
):
    core = lax.axis_index("c")
    chips = lax.axis_size("yx")
    experts = 2 * chips
    tok_dev, width = tokens.shape
    capacity = 3 * tok_dev * TOP // (2 * experts)
    slots = experts * capacity
    hidden_all = w_gate.shape[2]
    half = hidden_all // 2
    rows_in = w_gate.shape[1]

    teacher_rows = lax.all_gather(critic_teacher, EP, axis=0, tiled=True)
    here = lax.axis_index("grp").astype(jnp.int32).reshape(1)
    pieces = ring_gather(pack_weights(w_gate[0], w_up[0], w_down[0]))

    meta = jnp.concatenate([expert_ids.T.astype(F32), route_weights.T])
    tok2 = both(core, tokens, swap(tokens)).reshape(2 * tok_dev, width)
    meta2 = both(core, meta, swap(meta))
    ids = meta2[:, :TOP].astype(jnp.int32)
    weights = meta2[:, TOP:]
    member = ids[:, :, None, :] == jnp.arange(experts, dtype=jnp.int32)[None, None, :, None]
    count = jnp.sum(member.astype(F32), axis=1).astype(BF)
    order = jnp.arange(tok_dev)
    earlier = (order[:, None] < order[None, :]).astype(BF)
    before = lax.dot_general(count, earlier, (((2,), (0,)), ((), ())), preferred_element_type=F32)
    rank = jnp.sum(jnp.where(member, before[:, None], 0.0), axis=2).astype(jnp.int32)
    source = jnp.arange(2, dtype=jnp.int32)[:, None, None]
    place = (ids // 2) * (2 * capacity) + source * capacity + rank
    place = jnp.where(ids % 2 == core, place, -1)
    place = place.transpose(1, 0, 2).reshape(TOP, 2 * tok_dev)
    weights = weights.transpose(1, 0, 2).reshape(TOP, 2 * tok_dev)
    hits = place[:, None, :] == jnp.arange(slots, dtype=jnp.int32)[None, :, None]
    pick = jnp.sum(hits.astype(F32), axis=0).astype(BF)
    scaled = jnp.sum(jnp.where(hits, weights[:, None, :], 0.0), axis=0)
    row_weight = jnp.sum(scaled, axis=1)
    scaled_high, scaled_low = split(scaled)

    outbound = dot(pick, tok2).astype(BF).reshape(chips, 2 * capacity, width)
    rows_st = critic_student.shape[0]
    outbound = jnp.concatenate(
        [outbound, jnp.broadcast_to(critic_student[None], (chips, rows_st, width))], axis=1
    )
    inbound = lax.all_to_all(outbound, "yx", split_axis=0, concat_axis=0, tiled=True)
    routed = inbound[:, : 2 * capacity].reshape(slots, width)
    student_half = inbound[:, 2 * capacity :]
    student_rows = (
        both(core, student_half, swap(student_half)).transpose(1, 0, 2, 3).reshape(width, -1)
    )

    hidden, coef_gate, coef_up, expert_out = expert_forward(here, routed, pieces, rows_in)
    returned = lax.all_to_all(
        expert_out.reshape(chips, 2 * capacity, width),
        "yx",
        split_axis=0,
        concat_axis=0,
        tiled=True,
    ).reshape(slots, width)

    partial = dot(scaled_high, returned, ((0,), (0,))) + dot(scaled_low, returned, ((0,), (0,)))
    partial = partial.reshape(2, tok_dev, width)
    mine = lax.dynamic_index_in_dim(partial, core, 0, keepdims=False)
    theirs = lax.dynamic_index_in_dim(partial, 1 - core, 0, keepdims=False)
    student = (mine + swap(theirs)).astype(BF)
    pre_teacher = dot(teacher, teacher_rows)
    pre = pre_teacher + dot(student, student_rows)
    score = jnp.sum(gelu_tanh(pre) * critic_head[None, :], axis=1)
    dscore = -jax.nn.sigmoid(-score)
    dpre = (dscore[:, None] * critic_head[None, :] * gelu_slope(pre)).astype(BF)
    dpre2 = both(core, dpre, swap(dpre)).reshape(2 * tok_dev, -1)
    dstudent = dot(dpre2, student_rows, ((1,), (1,)))
    ds_high, ds_low = split(dstudent)
    grad_rows = dot(pick, ds_high) + dot(pick, ds_low)
    grad_out = (grad_rows * row_weight[:, None]).astype(BF)
    droute = lax.all_to_all(
        grad_out.reshape(chips, 2 * capacity, width), "yx", split_axis=0, concat_axis=0, tiled=True
    ).reshape(slots, width)

    parts = expert_backward(here, droute, routed, hidden, coef_gate, coef_up, pieces, rows_in)
    total = lax.psum_scatter(
        parts.reshape(-1, width), "grp", scatter_dimension=0, tiled=True
    )
    grad_gate, grad_up, grad_down = unpack_grads(total, rows_in, half)
    return (grad_gate[None], grad_up[None], grad_down[None], score)


def solution(mesh):
    groups, members = mesh.devices.shape
    fine = Mesh(mesh.devices.reshape(groups, members // 2, 2), ("grp",) + EP)
    rows = P(("grp",) + EP, None)
    weights = P(EP, "grp", None)
    critic = P(EP, None)
    in_specs = (rows, rows, rows, rows, weights, weights, weights, critic, critic, P())
    out_specs = (weights, weights, weights, P(("grp",) + EP))
    return jax.shard_map(layer, mesh=fine, in_specs=in_specs, out_specs=out_specs, check_vma=False)
```

```python
import functools
import math

import jax
import jax.numpy as jnp
from jax import lax
from jax.experimental import pallas as pl
from jax.experimental.pallas import tpu as pltpu
from jax.sharding import Mesh
from jax.sharding import PartitionSpec as P

TOP = 4
CHIPS = ("y", "x")
ROW = ("x", "c")
EP = ("y", "x", "c")
BF = jnp.bfloat16
F32 = jnp.float32


def gelu_tanh(value):
    inner = 0.7978845608 * (value + 0.044715 * value * value * value)
    return 0.5 * value * (1.0 + jnp.tanh(inner))


def gelu_slope(value):
    inner = 0.7978845608 * (value + 0.044715 * value * value * value)
    tangent = jnp.tanh(inner)
    return 0.5 * (1.0 + tangent) + 0.5 * value * (1.0 - tangent * tangent) * 0.7978845608 * (
        1.0 + 3.0 * 0.044715 * value * value
    )


def dot(left, right, dims=((1,), (0,))):
    return lax.dot_general(left, right, (dims, ((), ())), preferred_element_type=F32)


def split(value):
    high = value.astype(BF)
    return high, (value - high.astype(F32)).astype(BF)


def shift(value, axis, step):
    count = lax.axis_size(axis)
    return lax.ppermute(value, axis, [(i, (i + step) % count) for i in range(count)])


def swap(value):
    return shift(value, "c", 1)


def both(core, own, other):
    first = core == 0
    return jnp.stack([jnp.where(first, own, other), jnp.where(first, other, own)])


VMEM = pl.BlockSpec(memory_space=pltpu.VMEM)
SMEM = pl.BlockSpec(memory_space=pltpu.SMEM)
ANY = pl.BlockSpec(memory_space=pl.ANY)


def pack_kernel(gate_ref, up_ref, down_ref, out_ref):
    rows, hidden = gate_ref.shape
    half = hidden // 2
    out_ref[0:rows] = gate_ref[:, :half]
    out_ref[rows : 2 * rows] = gate_ref[:, half:]
    out_ref[2 * rows : 3 * rows] = up_ref[:, :half]
    out_ref[3 * rows : 4 * rows] = up_ref[:, half:]
    out_ref[4 * rows :] = down_ref[...]


def pack_weights(gate, up, down):
    rows = 4 * gate.shape[0] + down.shape[0]
    return pl.pallas_call(
        pack_kernel,
        out_shape=jax.ShapeDtypeStruct((rows, down.shape[1]), BF),
        in_specs=[VMEM] * 3,
        out_specs=VMEM,
        name="pack",
    )(gate, up, down)


def unpack_kernel(in_ref, gate_ref, up_ref, down_ref):
    rows, hidden = gate_ref.shape
    half = hidden // 2
    gate_ref[:, :half] = in_ref[0:rows].astype(F32)
    gate_ref[:, half:] = in_ref[rows : 2 * rows].astype(F32)
    up_ref[:, :half] = in_ref[2 * rows : 3 * rows].astype(F32)
    up_ref[:, half:] = in_ref[3 * rows : 4 * rows].astype(F32)
    down_ref[...] = in_ref[4 * rows :].astype(F32)


def unpack_grads(total, rows, half):
    return pl.pallas_call(
        unpack_kernel,
        out_shape=[
            jax.ShapeDtypeStruct((rows, 2 * half), F32),
            jax.ShapeDtypeStruct((rows, 2 * half), F32),
            jax.ShapeDtypeStruct((total.shape[0] - 4 * rows, total.shape[1]), F32),
        ],
        in_specs=[VMEM],
        out_specs=[VMEM] * 3,
        name="unpack",
    )(total)


def forward_kernel(rows, routed_ref, full, hid_ref, coef_gate_ref, coef_up_ref, out_ref):
    count = full.shape[0]
    width = routed_ref.shape[1]
    half = full.shape[2]
    routed = routed_ref[...]
    out = jnp.zeros(out_ref.shape, F32)
    for part in range(2):
        gate_w = full[:, part * rows : (part + 1) * rows].reshape(width, half)
        up_w = full[:, (2 + part) * rows : (3 + part) * rows].reshape(width, half)
        gate = jnp.dot(routed, gate_w, preferred_element_type=F32)
        up = jnp.dot(routed, up_w, preferred_element_type=F32)
        sig = jax.nn.sigmoid(gate)
        silu = gate * sig
        hid = (silu * up).astype(BF)
        span = slice(part * half, (part + 1) * half)
        hid_ref[:, span] = hid
        coef_up_ref[:, span] = silu.astype(BF)
        coef_gate_ref[:, span] = (up * (sig + silu * (1.0 - sig))).astype(BF)
        group = count // 2
        down_w = full[part * group : (part + 1) * group, 4 * rows :].reshape(half, width)
        out += jnp.dot(hid, down_w, preferred_element_type=F32)
    out_ref[...] = out.astype(BF)


def expert_forward(routed, full, rows, tile=384):
    slots, width = routed.shape
    half = full.shape[2]
    hidden = 2 * half
    block = lambda cols: pl.BlockSpec((tile, cols), lambda i: (i, 0))
    wide = jax.ShapeDtypeStruct((slots, hidden), BF)
    return pl.pallas_call(
        functools.partial(forward_kernel, rows),
        grid=(slots // tile,),
        out_shape=[wide, wide, wide, jax.ShapeDtypeStruct((slots, width), BF)],
        in_specs=[block(width), pl.BlockSpec(full.shape, lambda i: (0, 0, 0))],
        out_specs=[block(hidden), block(hidden), block(hidden), block(width)],
        cost_estimate=pl.CostEstimate(
            flops=6 * slots * width * hidden,
            transcendentals=slots * hidden,
            bytes_accessed=6 * slots * hidden + 6 * width * hidden,
        ),
        name="expert_forward",
    )(routed, full)


def backward_kernel(
    rows, droute_ref, routed_ref, hid_ref, cg_ref, cu_ref, down, out_ref, parts, out_sems
):
    count = out_ref.shape[0]
    step = pl.program_id(0)
    width, half = routed_ref.shape[1], hid_ref.shape[1]
    each = down.shape[1]
    take = count // 2

    droute = droute_ref[...]
    routed = routed_ref[...]
    down_w = down[...].reshape(half, width)
    dhid = lax.dot_general(droute, down_w, (((1,), (1,)), ((), ())), preferred_element_type=F32)
    dgate = (dhid * cg_ref[...].astype(F32)).astype(BF)
    dup = (dhid * cu_ref[...].astype(F32)).astype(BF)
    rows_dot = functools.partial(
        lax.dot_general, dimension_numbers=(((0,), (0,)), ((), ())), preferred_element_type=F32
    )
    part_down = rows_dot(hid_ref[...], droute).astype(BF).reshape(take, each, width)
    part_gate = rows_dot(routed, dgate).astype(BF).reshape(count, rows, half)
    part_up = rows_dot(routed, dup).astype(BF).reshape(count, rows, half)

    def leaving(at):
        places = [(pl.ds(at * take, take), pl.ds(4 * rows, each))]
        places += [(slice(None), pl.ds(block * rows, rows)) for block in (at, 2 + at)]
        return [
            pltpu.make_async_copy(parts.at[place], out_ref.at[place], out_sems.at[3 * at + k])
            for k, place in enumerate(places)
        ]

    for at in range(2):

        @pl.when(step == at)
        def _():
            parts[at * take : (at + 1) * take, 4 * rows :] = part_down
            parts[:, at * rows : (at + 1) * rows] = part_gate
            parts[:, (2 + at) * rows : (3 + at) * rows] = part_up
            for copy in leaving(at):
                copy.start()

    @pl.when(step == 1)
    def _():
        for at in range(2):
            for copy in leaving(at):
                copy.wait()


def expert_backward(droute, routed, hid, coef_gate, coef_up, full, rows):
    slots, width = routed.shape
    hidden = hid.shape[1]
    whole = pl.BlockSpec((slots, width), lambda i: (0, 0))
    block = pl.BlockSpec((slots, hidden // 2), lambda i: (0, i))
    shape = full.shape
    each = shape[1] - 4 * rows
    down = pl.BlockSpec((shape[0] // 2, each, width), lambda i: (i, 4 * rows // each, 0))
    return pl.pallas_call(
        functools.partial(backward_kernel, rows),
        grid=(2,),
        out_shape=jax.ShapeDtypeStruct(shape, BF),
        in_specs=[whole, whole, block, block, block, down],
        out_specs=ANY,
        scratch_shapes=[
            pltpu.VMEM(shape, BF),
            pltpu.SemaphoreType.DMA((6,)),
        ],
        cost_estimate=pl.CostEstimate(
            flops=8 * slots * width * hidden,
            transcendentals=0,
            bytes_accessed=6 * slots * hidden + 6 * width * hidden,
        ),
        name="expert_backward",
    )(droute, routed, hid, coef_gate, coef_up, full)


def slice_kernel(in_ref, out_ref):
    out_ref[0] = in_ref[...]


def slice_features(teacher, side):
    tok_dev, depth = teacher.shape
    each = depth // side
    return pl.pallas_call(
        slice_kernel,
        grid=(side,),
        out_shape=jax.ShapeDtypeStruct((side, tok_dev, each), BF),
        in_specs=[pl.BlockSpec((tok_dev, each), lambda i: (0, i))],
        out_specs=pl.BlockSpec((1, tok_dev, each), lambda i: (i, 0, 0)),
        name="slice_features",
    )(teacher)


def share_teacher(slices):
    return lax.all_to_all(slices, ROW, split_axis=0, concat_axis=0, tiled=True)


def share_critic(critic_teacher):
    side = lax.axis_size("y")
    turn = [(i * side + j, j * side + i) for i in range(side) for j in range(side)]
    turned = lax.ppermute(critic_teacher, EP, turn)
    return lax.all_gather(turned, "y", axis=0, tiled=True)


def layer(
    tokens,
    teacher,
    expert_ids,
    route_weights,
    w_gate,
    w_up,
    w_down,
    critic_teacher,
    critic_student,
    critic_head,
):
    core = lax.axis_index("c")
    chips = lax.axis_size("y") * lax.axis_size("x")
    experts = 2 * chips
    tok_dev, width = tokens.shape
    capacity = 3 * tok_dev * TOP // (2 * experts)
    slots = experts * capacity
    hidden_all = w_gate.shape[2]
    half = hidden_all // 2
    rows_in = w_gate.shape[1]

    packed = pack_weights(w_gate[0], w_up[0], w_down[0])
    packed, teacher, tokens, expert_ids, critic_student = lax.optimization_barrier(
        (packed, teacher, tokens, expert_ids, critic_student)
    )
    full = lax.all_gather(packed, "grp", axis=0)
    theirs = share_teacher(slice_features(teacher, lax.axis_size("y")))
    student_half = lax.all_gather(critic_student, CHIPS, axis=0)
    student_rows = (
        both(core, student_half, swap(student_half)).transpose(1, 0, 2, 3).reshape(width, -1)
    )

    meta = jnp.concatenate([expert_ids.T.astype(F32), route_weights.T])
    tok2 = both(core, tokens, swap(tokens)).reshape(2 * tok_dev, width)
    meta2 = both(core, meta, swap(meta))
    ids = meta2[:, :TOP].astype(jnp.int32)
    weights = meta2[:, TOP:]
    member = ids[:, :, None, :] == jnp.arange(experts, dtype=jnp.int32)[None, None, :, None]
    count = jnp.sum(member.astype(F32), axis=1).astype(BF)
    order = jnp.arange(tok_dev)
    earlier = (order[:, None] < order[None, :]).astype(BF)
    before = lax.dot_general(count, earlier, (((2,), (0,)), ((), ())), preferred_element_type=F32)
    rank = jnp.sum(jnp.where(member, before[:, None], 0.0), axis=2).astype(jnp.int32)
    source = jnp.arange(2, dtype=jnp.int32)[:, None, None]
    place = (ids // 2) * (2 * capacity) + source * capacity + rank
    place = jnp.where(ids % 2 == core, place, -1)
    place = place.transpose(1, 0, 2).reshape(TOP, 2 * tok_dev)
    weights = weights.transpose(1, 0, 2).reshape(TOP, 2 * tok_dev)
    hits = place[:, None, :] == jnp.arange(slots, dtype=jnp.int32)[None, :, None]
    pick = jnp.sum(hits.astype(F32), axis=0).astype(BF)
    scaled = jnp.sum(jnp.where(hits, weights[:, None, :], 0.0), axis=0)
    row_weight = jnp.sum(scaled, axis=1)
    scaled_high, scaled_low = split(scaled)

    outbound = dot(pick, tok2).astype(BF).reshape(chips, 2 * capacity, width)
    outbound, theirs, student_rows = lax.optimization_barrier((outbound, theirs, student_rows))
    inbound = lax.all_to_all(outbound, CHIPS, split_axis=0, concat_axis=0, tiled=True)
    critic_rows = share_critic(critic_teacher)
    product = dot(theirs.reshape(-1, theirs.shape[2]), critic_rows).astype(BF)
    inbound, product = lax.optimization_barrier((inbound, product))
    pre_teacher = lax.psum_scatter(product, ROW, scatter_dimension=0, tiled=True)
    pre_teacher = pre_teacher.astype(F32)
    routed = inbound.reshape(slots, width)

    hidden, coef_gate, coef_up, expert_out = expert_forward(routed, full, rows_in)
    returned = lax.all_to_all(
        expert_out.reshape(chips, 2 * capacity, width), CHIPS, split_axis=0, concat_axis=0, tiled=True
    ).reshape(slots, width)

    partial = dot(scaled_high, returned, ((0,), (0,))) + dot(scaled_low, returned, ((0,), (0,)))
    partial = partial.reshape(2, tok_dev, width)
    mine = lax.dynamic_index_in_dim(partial, core, 0, keepdims=False)
    theirs = lax.dynamic_index_in_dim(partial, 1 - core, 0, keepdims=False)
    student = (mine + swap(theirs)).astype(BF)
    pre = pre_teacher + dot(student, student_rows)
    score = jnp.sum(gelu_tanh(pre) * critic_head[None, :], axis=1)
    dscore = -jax.nn.sigmoid(-score)
    dpre = (dscore[:, None] * critic_head[None, :] * gelu_slope(pre)).astype(BF)
    dpre2 = both(core, dpre, swap(dpre)).reshape(2 * tok_dev, -1)
    dstudent = dot(dpre2, student_rows, ((1,), (1,)))
    ds_high, ds_low = split(dstudent)
    grad_rows = dot(pick, ds_high) + dot(pick, ds_low)
    grad_out = (grad_rows * row_weight[:, None]).astype(BF)
    droute = lax.all_to_all(
        grad_out.reshape(chips, 2 * capacity, width), CHIPS, split_axis=0, concat_axis=0, tiled=True
    ).reshape(slots, width)

    parts = expert_backward(droute, routed, hidden, coef_gate, coef_up, full, rows_in)
    total = lax.psum_scatter(
        parts.reshape(-1, width), "grp", scatter_dimension=0, tiled=True
    )
    grad_gate, grad_up, grad_down = unpack_grads(total, rows_in, half)
    return (grad_gate[None], grad_up[None], grad_down[None], score)


def solution(mesh):
    groups, members = mesh.devices.shape
    side = math.isqrt(members)
    fine = Mesh(mesh.devices.reshape(groups, side, side // 2, 2), ("grp",) + EP)
    rows = P(("grp",) + EP, None)
    weights = P(EP, "grp", None)
    critic = P(EP, None)
    in_specs = (rows, rows, rows, rows, weights, weights, weights, critic, critic, P())
    out_specs = (weights, weights, weights, P(("grp",) + EP))
    return jax.shard_map(layer, mesh=fine, in_specs=in_specs, out_specs=out_specs, check_vma=False)
```

```python
import functools

import jax
import jax.numpy as jnp
from jax import lax
from jax.experimental import pallas as pl
from jax.experimental.pallas import tpu as pltpu
from jax.sharding import Mesh
from jax.sharding import PartitionSpec as P

TOP = 4
CHIPS = ("y", "x")
EP = ("y", "x", "c")
BF = jnp.bfloat16
F32 = jnp.float32


def gelu_tanh(value):
    inner = 0.7978845608 * (value + 0.044715 * value * value * value)
    return 0.5 * value * (1.0 + jnp.tanh(inner))


def gelu_slope(value):
    inner = 0.7978845608 * (value + 0.044715 * value * value * value)
    tangent = jnp.tanh(inner)
    return 0.5 * (1.0 + tangent) + 0.5 * value * (1.0 - tangent * tangent) * 0.7978845608 * (
        1.0 + 3.0 * 0.044715 * value * value
    )


def dot(left, right, dims=((1,), (0,))):
    return lax.dot_general(left, right, (dims, ((), ())), preferred_element_type=F32)


def split(value):
    high = value.astype(BF)
    return high, (value - high.astype(F32)).astype(BF)


def shift(value, axis, step):
    count = lax.axis_size(axis)
    return lax.ppermute(value, axis, [(i, (i + step) % count) for i in range(count)])


def swap(value):
    return shift(value, "c", 1)


def both(core, own, other):
    first = core == 0
    return jnp.stack([jnp.where(first, own, other), jnp.where(first, other, own)])


VMEM = pl.BlockSpec(memory_space=pltpu.VMEM)
SMEM = pl.BlockSpec(memory_space=pltpu.SMEM)
ANY = pl.BlockSpec(memory_space=pl.ANY)


def pack_kernel(gate_ref, up_ref, down_ref, out_ref):
    rows, hidden = gate_ref.shape
    half = hidden // 2
    out_ref[0:rows] = gate_ref[:, :half]
    out_ref[rows : 2 * rows] = gate_ref[:, half:]
    out_ref[2 * rows : 3 * rows] = up_ref[:, :half]
    out_ref[3 * rows : 4 * rows] = up_ref[:, half:]
    out_ref[4 * rows :] = down_ref[...]


def pack_weights(gate, up, down):
    rows = 4 * gate.shape[0] + down.shape[0]
    return pl.pallas_call(
        pack_kernel,
        out_shape=jax.ShapeDtypeStruct((rows, down.shape[1]), BF),
        in_specs=[VMEM] * 3,
        out_specs=VMEM,
        name="pack",
    )(gate, up, down)


def unpack_kernel(in_ref, gate_ref, up_ref, down_ref):
    rows, hidden = gate_ref.shape
    half = hidden // 2
    gate_ref[:, :half] = in_ref[0:rows].astype(F32)
    gate_ref[:, half:] = in_ref[rows : 2 * rows].astype(F32)
    up_ref[:, :half] = in_ref[2 * rows : 3 * rows].astype(F32)
    up_ref[:, half:] = in_ref[3 * rows : 4 * rows].astype(F32)
    down_ref[...] = in_ref[4 * rows :].astype(F32)


def unpack_grads(total, rows, half):
    return pl.pallas_call(
        unpack_kernel,
        out_shape=[
            jax.ShapeDtypeStruct((rows, 2 * half), F32),
            jax.ShapeDtypeStruct((rows, 2 * half), F32),
            jax.ShapeDtypeStruct((total.shape[0] - 4 * rows, total.shape[1]), F32),
        ],
        in_specs=[VMEM],
        out_specs=[VMEM] * 3,
        name="unpack",
    )(total)


def forward_kernel(rows, routed_ref, full, hid_ref, coef_gate_ref, coef_up_ref, out_ref):
    count = full.shape[0]
    width = routed_ref.shape[1]
    half = full.shape[2]
    routed = routed_ref[...]
    out = jnp.zeros(out_ref.shape, F32)
    for part in range(2):
        gate_w = full[:, part * rows : (part + 1) * rows].reshape(width, half)
        up_w = full[:, (2 + part) * rows : (3 + part) * rows].reshape(width, half)
        gate = jnp.dot(routed, gate_w, preferred_element_type=F32)
        up = jnp.dot(routed, up_w, preferred_element_type=F32)
        sig = jax.nn.sigmoid(gate)
        silu = gate * sig
        hid = (silu * up).astype(BF)
        span = slice(part * half, (part + 1) * half)
        hid_ref[:, span] = hid
        coef_up_ref[:, span] = silu.astype(BF)
        coef_gate_ref[:, span] = (up * (sig + silu * (1.0 - sig))).astype(BF)
        group = count // 2
        down_w = full[part * group : (part + 1) * group, 4 * rows :].reshape(half, width)
        out += jnp.dot(hid, down_w, preferred_element_type=F32)
    out_ref[...] = out.astype(BF)


def expert_forward(routed, full, rows, tile=384):
    slots, width = routed.shape
    half = full.shape[2]
    hidden = 2 * half
    block = lambda cols: pl.BlockSpec((tile, cols), lambda i: (i, 0))
    wide = jax.ShapeDtypeStruct((slots, hidden), BF)
    return pl.pallas_call(
        functools.partial(forward_kernel, rows),
        grid=(slots // tile,),
        out_shape=[wide, wide, wide, jax.ShapeDtypeStruct((slots, width), BF)],
        in_specs=[block(width), pl.BlockSpec(full.shape, lambda i: (0, 0, 0))],
        out_specs=[block(hidden), block(hidden), block(hidden), block(width)],
        cost_estimate=pl.CostEstimate(
            flops=6 * slots * width * hidden,
            transcendentals=slots * hidden,
            bytes_accessed=6 * slots * hidden + 6 * width * hidden,
        ),
        name="expert_forward",
    )(routed, full)


def backward_kernel(
    rows, droute_ref, routed_ref, hid_ref, cg_ref, cu_ref, down, out_ref, parts, out_sems
):
    count = out_ref.shape[0]
    step = pl.program_id(0)
    width, half = routed_ref.shape[1], hid_ref.shape[1]
    each = down.shape[1]
    take = count // 2

    droute = droute_ref[...]
    routed = routed_ref[...]
    down_w = down[...].reshape(half, width)
    dhid = lax.dot_general(droute, down_w, (((1,), (1,)), ((), ())), preferred_element_type=F32)
    dgate = (dhid * cg_ref[...].astype(F32)).astype(BF)
    dup = (dhid * cu_ref[...].astype(F32)).astype(BF)
    rows_dot = functools.partial(
        lax.dot_general, dimension_numbers=(((0,), (0,)), ((), ())), preferred_element_type=F32
    )
    part_down = rows_dot(hid_ref[...], droute).astype(BF).reshape(take, each, width)
    part_gate = rows_dot(routed, dgate).astype(BF).reshape(count, rows, half)
    part_up = rows_dot(routed, dup).astype(BF).reshape(count, rows, half)

    def leaving(at):
        places = [(pl.ds(at * take, take), pl.ds(4 * rows, each))]
        places += [(slice(None), pl.ds(block * rows, rows)) for block in (at, 2 + at)]
        return [
            pltpu.make_async_copy(parts.at[place], out_ref.at[place], out_sems.at[3 * at + k])
            for k, place in enumerate(places)
        ]

    for at in range(2):

        @pl.when(step == at)
        def _():
            parts[at * take : (at + 1) * take, 4 * rows :] = part_down
            parts[:, at * rows : (at + 1) * rows] = part_gate
            parts[:, (2 + at) * rows : (3 + at) * rows] = part_up
            for copy in leaving(at):
                copy.start()

    @pl.when(step == 1)
    def _():
        for at in range(2):
            for copy in leaving(at):
                copy.wait()


def expert_backward(droute, routed, hid, coef_gate, coef_up, full, rows):
    slots, width = routed.shape
    hidden = hid.shape[1]
    whole = pl.BlockSpec((slots, width), lambda i: (0, 0))
    block = pl.BlockSpec((slots, hidden // 2), lambda i: (0, i))
    shape = full.shape
    each = shape[1] - 4 * rows
    down = pl.BlockSpec((shape[0] // 2, each, width), lambda i: (i, 4 * rows // each, 0))
    return pl.pallas_call(
        functools.partial(backward_kernel, rows),
        grid=(2,),
        out_shape=jax.ShapeDtypeStruct(shape, BF),
        in_specs=[whole, whole, block, block, block, down],
        out_specs=ANY,
        scratch_shapes=[
            pltpu.VMEM(shape, BF),
            pltpu.SemaphoreType.DMA((6,)),
        ],
        cost_estimate=pl.CostEstimate(
            flops=8 * slots * width * hidden,
            transcendentals=0,
            bytes_accessed=6 * slots * hidden + 6 * width * hidden,
        ),
        name="expert_backward",
    )(droute, routed, hid, coef_gate, coef_up, full)


def ring(block, axis):
    count = lax.axis_size(axis)
    pieces = [block] + [None] * (count - 1)
    up = down = block
    for step in range(1, count // 2 + 1):
        up = shift(up, axis, 1)
        pieces[step] = up
        if 2 * step < count:
            down = shift(down, axis, -1)
            pieces[count - step] = down
    return pieces


def order_kernel(here_ref, *refs):
    count = len(refs) - 1
    for k in range(count):
        refs[count][lax.rem(here_ref[0] - k + count, count)] = refs[k][...]


def in_order(here, pieces):
    return pl.pallas_call(
        order_kernel,
        out_shape=jax.ShapeDtypeStruct((len(pieces),) + pieces[0].shape, BF),
        in_specs=[SMEM] + [VMEM] * len(pieces),
        out_specs=VMEM,
        name="in_order",
    )(here, *pieces)


def critic_kernel(
    tall, here_ref, own_ref, other_ref, block, behind, ahead, low, high,
    out_ref, student_ref, tokens, rows, sems, row_sems,
):
    tok_dev = own_ref.shape[0]
    columns, deep = rows.shape[:2]
    half = deep // 2
    at = lambda k: lax.rem(here_ref[0] + k, columns)
    copies = [
        pltpu.make_async_copy(own_ref, tokens.at[pl.ds(0, tok_dev)], sems.at[0]),
        pltpu.make_async_copy(other_ref, tokens.at[pl.ds(tok_dev, tok_dev)], sems.at[1]),
        pltpu.make_async_copy(block, rows.at[at(0)], row_sems.at[0]),
        pltpu.make_async_copy(behind, rows.at[at(3)], row_sems.at[1]),
        pltpu.make_async_copy(ahead, rows.at[at(1)], row_sems.at[2]),
        pltpu.make_async_copy(low, rows.at[at(2), pl.ds(0, half)], row_sems.at[3]),
        pltpu.make_async_copy(high, rows.at[at(2), pl.ds(half, half)], row_sems.at[4]),
    ]
    for copy in copies:
        copy.start()
    for copy in copies:
        copy.wait()
    span = columns * tall
    cols = rows.shape[3]
    small = columns * (rows.shape[2] - tall)
    total = jnp.zeros((2 * tok_dev, cols), F32)
    for y in range(deep):
        weights = rows[:, y, :tall].reshape(span, cols)
        total += jnp.dot(
            tokens[:, y * span : (y + 1) * span], weights, preferred_element_type=F32
        )
        student_ref[y * small : (y + 1) * small] = rows[:, y, tall:].reshape(small, cols)
    out_ref[0] = total[:tok_dev]
    out_ref[1] = total[tok_dev:]


def critic_product(here, own, other, pieces, tall):
    block = pieces[0]
    deep, high, cols = block.shape
    tok_dev, depth = own.shape
    columns = 4
    return pl.pallas_call(
        functools.partial(critic_kernel, tall),
        out_shape=[
            jax.ShapeDtypeStruct((2, tok_dev, cols), F32),
            jax.ShapeDtypeStruct((columns * deep * (high - tall), cols), BF),
        ],
        in_specs=[SMEM] + [ANY] * 7,
        out_specs=[VMEM] * 2,
        scratch_shapes=[
            pltpu.VMEM((2 * tok_dev, depth), BF),
            pltpu.VMEM((columns,) + block.shape, BF),
            pltpu.SemaphoreType.DMA((2,)),
            pltpu.SemaphoreType.DMA((5,)),
        ],
        cost_estimate=pl.CostEstimate(
            flops=4 * tok_dev * depth * cols,
            transcendentals=0,
            bytes_accessed=4 * tok_dev * depth + 2 * depth * cols,
        ),
        name="critic_product",
    )(here, own, other, *pieces)


def columns_of(core, value, which):
    size = value.shape[1] // 2
    at = core if which == 0 else 1 - core
    return lax.dynamic_slice_in_dim(value, at * size, size, axis=1)


def side_by_side(core, own, other):
    first = core == 0
    return jnp.concatenate(
        [jnp.where(first, own, other), jnp.where(first, other, own)], axis=1
    )


def critic_on_teacher(core, teacher, critic_teacher, critic_student):
    shard = jnp.concatenate([critic_teacher, critic_student])
    mine = columns_of(core, shard, 0)
    got = swap(columns_of(core, shard, 1))
    pair = both(core, mine, got)
    depth, cols = critic_teacher.shape[0], pair.shape[2]
    block = jnp.concatenate(
        [pair[:, :depth].reshape(-1, cols), pair[:, depth:].reshape(-1, cols)]
    )
    other = swap(teacher)
    place = lambda axis: lax.axis_index(axis).astype(jnp.int32).reshape(1)
    column = in_order(place("y"), ring(block, "y"))
    cut = column.shape[0] // 2
    behind = shift(column, "x", 1)
    ahead = shift(column, "x", -1)
    low = shift(behind[:cut], "x", 1)
    high = shift(ahead[cut:], "x", -1)
    product, student = critic_product(
        place("x"), teacher, other, [column, behind, ahead, low, high], 2 * depth
    )
    pre = side_by_side(core, product[0], swap(product[1]))
    student = side_by_side(core, student, swap(student))
    return pre, student


def layer(
    tokens,
    teacher,
    expert_ids,
    route_weights,
    w_gate,
    w_up,
    w_down,
    critic_teacher,
    critic_student,
    critic_head,
):
    core = lax.axis_index("c")
    chips = lax.axis_size("y") * lax.axis_size("x")
    experts = 2 * chips
    tok_dev, width = tokens.shape
    capacity = 3 * tok_dev * TOP // (2 * experts)
    slots = experts * capacity
    hidden_all = w_gate.shape[2]
    half = hidden_all // 2
    rows_in = w_gate.shape[1]

    packed = pack_weights(w_gate[0], w_up[0], w_down[0])
    packed, teacher, tokens, expert_ids = lax.optimization_barrier(
        (packed, teacher, tokens, expert_ids)
    )
    full = lax.all_gather(packed, "grp", axis=0)
    pre_teacher, student_rows = critic_on_teacher(core, teacher, critic_teacher, critic_student)

    meta = jnp.concatenate([expert_ids.T.astype(F32), route_weights.T])
    tok2 = both(core, tokens, swap(tokens)).reshape(2 * tok_dev, width)
    meta2 = both(core, meta, swap(meta))
    ids = meta2[:, :TOP].astype(jnp.int32)
    weights = meta2[:, TOP:]
    member = ids[:, :, None, :] == jnp.arange(experts, dtype=jnp.int32)[None, None, :, None]
    count = jnp.sum(member.astype(F32), axis=1).astype(BF)
    order = jnp.arange(tok_dev)
    earlier = (order[:, None] < order[None, :]).astype(BF)
    before = lax.dot_general(count, earlier, (((2,), (0,)), ((), ())), preferred_element_type=F32)
    rank = jnp.sum(jnp.where(member, before[:, None], 0.0), axis=2).astype(jnp.int32)
    source = jnp.arange(2, dtype=jnp.int32)[:, None, None]
    place = (ids // 2) * (2 * capacity) + source * capacity + rank
    place = jnp.where(ids % 2 == core, place, -1)
    place = place.transpose(1, 0, 2).reshape(TOP, 2 * tok_dev)
    weights = weights.transpose(1, 0, 2).reshape(TOP, 2 * tok_dev)
    hits = place[:, None, :] == jnp.arange(slots, dtype=jnp.int32)[None, :, None]
    pick = jnp.sum(hits.astype(F32), axis=0).astype(BF)
    scaled = jnp.sum(jnp.where(hits, weights[:, None, :], 0.0), axis=0)
    row_weight = jnp.sum(scaled, axis=1)
    scaled_high, scaled_low = split(scaled)

    outbound = dot(pick, tok2).astype(BF).reshape(chips, 2 * capacity, width)
    inbound = lax.all_to_all(outbound, CHIPS, split_axis=0, concat_axis=0, tiled=True)
    routed = inbound.reshape(slots, width)

    hidden, coef_gate, coef_up, expert_out = expert_forward(routed, full, rows_in)
    returned = lax.all_to_all(
        expert_out.reshape(chips, 2 * capacity, width), CHIPS, split_axis=0, concat_axis=0, tiled=True
    ).reshape(slots, width)

    partial = dot(scaled_high, returned, ((0,), (0,))) + dot(scaled_low, returned, ((0,), (0,)))
    partial = partial.reshape(2, tok_dev, width)
    mine = lax.dynamic_index_in_dim(partial, core, 0, keepdims=False)
    theirs = lax.dynamic_index_in_dim(partial, 1 - core, 0, keepdims=False)
    student = (mine + swap(theirs)).astype(BF)
    pre = pre_teacher + dot(student, student_rows)
    score = jnp.sum(gelu_tanh(pre) * critic_head[None, :], axis=1)
    dscore = -jax.nn.sigmoid(-score)
    dpre = (dscore[:, None] * critic_head[None, :] * gelu_slope(pre)).astype(BF)
    dpre2 = both(core, dpre, swap(dpre)).reshape(2 * tok_dev, -1)
    dstudent = dot(dpre2, student_rows, ((1,), (1,)))
    ds_high, ds_low = split(dstudent)
    grad_rows = dot(pick, ds_high) + dot(pick, ds_low)
    grad_out = (grad_rows * row_weight[:, None]).astype(BF)
    droute = lax.all_to_all(
        grad_out.reshape(chips, 2 * capacity, width), CHIPS, split_axis=0, concat_axis=0, tiled=True
    ).reshape(slots, width)

    parts = expert_backward(droute, routed, hidden, coef_gate, coef_up, full, rows_in)
    total = lax.psum_scatter(
        parts.reshape(-1, width), "grp", scatter_dimension=0, tiled=True
    )
    grad_gate, grad_up, grad_down = unpack_grads(total, rows_in, half)
    return (grad_gate[None], grad_up[None], grad_down[None], score)


def solution(mesh):
    groups, members = mesh.devices.shape
    fine = Mesh(mesh.devices.reshape(groups, members // 8, 4, 2), ("grp",) + EP)
    rows = P(("grp",) + EP, None)
    weights = P(EP, "grp", None)
    critic = P(EP, None)
    in_specs = (rows, rows, rows, rows, weights, weights, weights, critic, critic, P())
    out_specs = (weights, weights, weights, P(("grp",) + EP))
    return jax.shard_map(layer, mesh=fine, in_specs=in_specs, out_specs=out_specs, check_vma=False)
```

```python
import functools

import jax
import jax.numpy as jnp
from jax import lax
from jax.experimental import pallas as pl
from jax.experimental.pallas import tpu as pltpu
from jax.sharding import Mesh
from jax.sharding import PartitionSpec as P

TOP = 4
EP = ("yx", "c")
BF = jnp.bfloat16
F32 = jnp.float32


def gelu_tanh(value):
    inner = 0.7978845608 * (value + 0.044715 * value * value * value)
    return 0.5 * value * (1.0 + jnp.tanh(inner))


def gelu_slope(value):
    inner = 0.7978845608 * (value + 0.044715 * value * value * value)
    tangent = jnp.tanh(inner)
    return 0.5 * (1.0 + tangent) + 0.5 * value * (1.0 - tangent * tangent) * 0.7978845608 * (
        1.0 + 3.0 * 0.044715 * value * value
    )


def dot(left, right, dims=((1,), (0,))):
    return lax.dot_general(left, right, (dims, ((), ())), preferred_element_type=F32)


def split(value):
    high = value.astype(BF)
    return high, (value - high.astype(F32)).astype(BF)


def shift(value, axis, step):
    count = lax.axis_size(axis)
    return lax.ppermute(value, axis, [(i, (i + step) % count) for i in range(count)])


def swap(value):
    return shift(value, "c", 1)


def both(core, own, other):
    first = core == 0
    return jnp.stack([jnp.where(first, own, other), jnp.where(first, other, own)])


def ring_gather(block):
    count = lax.axis_size("grp")
    pieces = [block] + [None] * (count - 1)
    up = down = block
    for step in range(1, count // 2 + 1):
        up = shift(up, "grp", 1)
        pieces[step] = up
        if 2 * step < count:
            down = shift(down, "grp", -1)
            pieces[count - step] = down
    return pieces


VMEM = pl.BlockSpec(memory_space=pltpu.VMEM)
SMEM = pl.BlockSpec(memory_space=pltpu.SMEM)
ANY = pl.BlockSpec(memory_space=pl.ANY)


def pack_kernel(gate_ref, up_ref, down_ref, out_ref):
    rows, hidden = gate_ref.shape
    half = hidden // 2
    out_ref[0:rows] = gate_ref[:, :half]
    out_ref[rows : 2 * rows] = gate_ref[:, half:]
    out_ref[2 * rows : 3 * rows] = up_ref[:, :half]
    out_ref[3 * rows : 4 * rows] = up_ref[:, half:]
    out_ref[4 * rows :] = down_ref[...]


def pack_weights(gate, up, down):
    rows = 4 * gate.shape[0] + down.shape[0]
    return pl.pallas_call(
        pack_kernel,
        out_shape=jax.ShapeDtypeStruct((rows, down.shape[1]), BF),
        in_specs=[VMEM] * 3,
        out_specs=VMEM,
        name="pack",
    )(gate, up, down)


def unpack_kernel(in_ref, gate_ref, up_ref, down_ref):
    rows, hidden = gate_ref.shape
    half = hidden // 2
    gate_ref[:, :half] = in_ref[0:rows].astype(F32)
    gate_ref[:, half:] = in_ref[rows : 2 * rows].astype(F32)
    up_ref[:, :half] = in_ref[2 * rows : 3 * rows].astype(F32)
    up_ref[:, half:] = in_ref[3 * rows : 4 * rows].astype(F32)
    down_ref[...] = in_ref[4 * rows :].astype(F32)


def unpack_grads(total, rows, half):
    return pl.pallas_call(
        unpack_kernel,
        out_shape=[
            jax.ShapeDtypeStruct((rows, 2 * half), F32),
            jax.ShapeDtypeStruct((rows, 2 * half), F32),
            jax.ShapeDtypeStruct((total.shape[0] - 4 * rows, total.shape[1]), F32),
        ],
        in_specs=[VMEM],
        out_specs=[VMEM] * 3,
        name="unpack",
    )(total)


def fetch(count, here_ref, pieces, target, sems, first):
    copies = []
    for k in range(count):
        at = lax.rem(here_ref[0] - k + count, count)
        piece = pieces[k].at[pl.ds(first, target.shape[1])]
        copies.append(pltpu.make_async_copy(piece, target.at[at], sems.at[k]))
    return copies


def forward_kernel(count, rows, chunk, here_ref, inbound_ref, *refs):
    pieces = refs[:count]
    hid_ref, coef_gate_ref, coef_up_ref, out_ref, down_ref, full, sems = refs[count:]

    @pl.when(pl.program_id(0) == 0)
    def _():
        copies = fetch(count, here_ref, pieces, full, sems, 0)
        for copy in copies:
            copy.start()
        for copy in copies:
            copy.wait()
        down_ref[...] = full[:, 4 * rows :]

    tile, width = out_ref.shape
    half = full.shape[2]
    routed = inbound_ref[:, :chunk].reshape(tile, width)
    out = jnp.zeros(out_ref.shape, F32)
    for part in range(2):
        gate_w = full[:, part * rows : (part + 1) * rows].reshape(width, half)
        up_w = full[:, (2 + part) * rows : (3 + part) * rows].reshape(width, half)
        gate = jnp.dot(routed, gate_w, preferred_element_type=F32)
        up = jnp.dot(routed, up_w, preferred_element_type=F32)
        sig = jax.nn.sigmoid(gate)
        silu = gate * sig
        hid = (silu * up).astype(BF)
        span = slice(part * half, (part + 1) * half)
        hid_ref[:, span] = hid
        coef_up_ref[:, span] = silu.astype(BF)
        coef_gate_ref[:, span] = (up * (sig + silu * (1.0 - sig))).astype(BF)
        group = count // 2
        down_w = full[part * group : (part + 1) * group, 4 * rows :].reshape(half, width)
        out += jnp.dot(hid, down_w, preferred_element_type=F32)
    out_ref[...] = out.astype(BF)


def expert_forward(here, inbound, pieces, rows, chunk, steps=2):
    count = len(pieces)
    chips, taken, width = inbound.shape
    slots = chips * chunk
    tile = slots // steps
    high, half = pieces[0].shape
    down = (count, high - 4 * rows, half)
    hidden = 2 * half
    block = lambda cols: pl.BlockSpec((tile, cols), lambda i: (i, 0))
    wide = jax.ShapeDtypeStruct((slots, hidden), BF)
    return pl.pallas_call(
        functools.partial(forward_kernel, count, rows, chunk),
        grid=(steps,),
        out_shape=[
            wide,
            wide,
            wide,
            jax.ShapeDtypeStruct((slots, width), BF),
            jax.ShapeDtypeStruct(down, BF),
        ],
        in_specs=[SMEM, pl.BlockSpec((chips // steps, taken, width), lambda i: (i, 0, 0))]
        + [ANY] * count,
        out_specs=[
            block(hidden),
            block(hidden),
            block(hidden),
            block(width),
            pl.BlockSpec(down, lambda i: (0, 0, 0)),
        ],
        scratch_shapes=[
            pltpu.VMEM((count,) + pieces[0].shape, BF),
            pltpu.SemaphoreType.DMA((count,)),
        ],
        cost_estimate=pl.CostEstimate(
            flops=6 * slots * width * hidden,
            transcendentals=slots * hidden,
            bytes_accessed=6 * slots * hidden + 6 * width * hidden,
        ),
        name="expert_forward",
    )(here, inbound, *pieces)


def backward_kernel(
    rows, chunk, droute_ref, inbound_ref, hid_ref, cg_ref, cu_ref, down, out_ref, parts, out_sems
):
    step = pl.program_id(0)
    slots, width = droute_ref.shape
    half = hid_ref.shape[1]
    count = out_ref.shape[0]
    each = down.shape[1]
    take = count // 2
    droute = droute_ref[...]
    routed = inbound_ref[:, :chunk].reshape(slots, width)
    down_w = down[...].reshape(half, width)
    dhid = lax.dot_general(droute, down_w, (((1,), (1,)), ((), ())), preferred_element_type=F32)
    dgate = (dhid * cg_ref[...].astype(F32)).astype(BF)
    dup = (dhid * cu_ref[...].astype(F32)).astype(BF)
    rows_dot = functools.partial(
        lax.dot_general, dimension_numbers=(((0,), (0,)), ((), ())), preferred_element_type=F32
    )
    part_down = rows_dot(hid_ref[...], droute).astype(BF).reshape(take, each, width)
    part_gate = rows_dot(routed, dgate).astype(BF).reshape(count, rows, half)
    part_up = rows_dot(routed, dup).astype(BF).reshape(count, rows, half)

    def leaving(at):
        places = [(pl.ds(at * take, take), pl.ds(4 * rows, each))]
        places += [(slice(None), pl.ds(block * rows, rows)) for block in (at, 2 + at)]
        return [
            pltpu.make_async_copy(parts.at[place], out_ref.at[place], out_sems.at[3 * at + k])
            for k, place in enumerate(places)
        ]

    for at in range(2):

        @pl.when(step == at)
        def _():
            parts[at * take : (at + 1) * take, 4 * rows :] = part_down
            parts[:, at * rows : (at + 1) * rows] = part_gate
            parts[:, (2 + at) * rows : (3 + at) * rows] = part_up
            for copy in leaving(at):
                copy.start()

    @pl.when(step == 1)
    def _():
        for at in range(2):
            for copy in leaving(at):
                copy.wait()


def expert_backward(droute, inbound, hid, coef_gate, coef_up, down, rows, chunk):
    slots, width = droute.shape
    hidden = hid.shape[1]
    block = pl.BlockSpec((slots, hidden // 2), lambda i: (0, i))
    count, each = down.shape[:2]
    shape = (count, 4 * rows + each, width)
    return pl.pallas_call(
        functools.partial(backward_kernel, rows, chunk),
        grid=(2,),
        out_shape=jax.ShapeDtypeStruct(shape, BF),
        in_specs=[
            pl.BlockSpec((slots, width), lambda i: (0, 0)),
            pl.BlockSpec(inbound.shape, lambda i: (0, 0, 0)),
            block,
            block,
            block,
            pl.BlockSpec((count // 2, each, width), lambda i: (i, 0, 0)),
        ],
        out_specs=ANY,
        scratch_shapes=[
            pltpu.VMEM(shape, BF),
            pltpu.SemaphoreType.DMA((6,)),
        ],
        cost_estimate=pl.CostEstimate(
            flops=8 * slots * width * hidden,
            transcendentals=0,
            bytes_accessed=6 * slots * hidden + 6 * width * hidden,
        ),
        name="expert_backward",
    )(droute, inbound, hid, coef_gate, coef_up, down)


def layer(
    tokens,
    teacher,
    expert_ids,
    route_weights,
    w_gate,
    w_up,
    w_down,
    critic_teacher,
    critic_student,
    critic_head,
):
    core = lax.axis_index("c")
    chips = lax.axis_size("yx")
    experts = 2 * chips
    tok_dev, width = tokens.shape
    capacity = 3 * tok_dev * TOP // (2 * experts)
    slots = experts * capacity
    hidden_all = w_gate.shape[2]
    half = hidden_all // 2
    rows_in = w_gate.shape[1]

    teacher_rows = lax.all_gather(critic_teacher, EP, axis=0, tiled=True)
    here = lax.axis_index("grp").astype(jnp.int32).reshape(1)
    pieces = ring_gather(pack_weights(w_gate[0], w_up[0], w_down[0]))

    meta = jnp.concatenate([expert_ids.T.astype(F32), route_weights.T])
    tok2 = both(core, tokens, swap(tokens)).reshape(2 * tok_dev, width)
    meta2 = both(core, meta, swap(meta))
    ids = meta2[:, :TOP].astype(jnp.int32)
    weights = meta2[:, TOP:]
    member = ids[:, :, None, :] == jnp.arange(experts, dtype=jnp.int32)[None, None, :, None]
    count = jnp.sum(member.astype(F32), axis=1).astype(BF)
    order = jnp.arange(tok_dev)
    earlier = (order[:, None] < order[None, :]).astype(BF)
    before = lax.dot_general(count, earlier, (((2,), (0,)), ((), ())), preferred_element_type=F32)
    rank = jnp.sum(jnp.where(member, before[:, None], 0.0), axis=2).astype(jnp.int32)
    source = jnp.arange(2, dtype=jnp.int32)[:, None, None]
    place = (ids // 2) * (2 * capacity) + source * capacity + rank
    place = jnp.where(ids % 2 == core, place, -1)
    place = place.transpose(1, 0, 2).reshape(TOP, 2 * tok_dev)
    weights = weights.transpose(1, 0, 2).reshape(TOP, 2 * tok_dev)
    hits = place[:, None, :] == jnp.arange(slots, dtype=jnp.int32)[None, :, None]
    pick = jnp.sum(hits.astype(F32), axis=0).astype(BF)
    scaled = jnp.sum(jnp.where(hits, weights[:, None, :], 0.0), axis=0)
    row_weight = jnp.sum(scaled, axis=1)
    scaled_high, scaled_low = split(scaled)

    outbound = dot(pick, tok2).astype(BF).reshape(chips, 2 * capacity, width)
    rows_st = critic_student.shape[0]
    outbound = jnp.concatenate(
        [outbound, jnp.broadcast_to(critic_student[None], (chips, rows_st, width))], axis=1
    )
    inbound = lax.all_to_all(outbound, "yx", split_axis=0, concat_axis=0, tiled=True)
    student_half = inbound[:, 2 * capacity :]
    student_other = swap(student_half)
    student_rows = (
        both(core, student_half, student_other).transpose(1, 0, 2, 3).reshape(width, -1)
    )

    hidden, coef_gate, coef_up, expert_out, down_w = expert_forward(
        here, inbound, pieces, rows_in, 2 * capacity
    )
    returned = lax.all_to_all(
        expert_out.reshape(chips, 2 * capacity, width),
        "yx",
        split_axis=0,
        concat_axis=0,
        tiled=True,
    ).reshape(slots, width)

    partial = dot(scaled_high, returned, ((0,), (0,))) + dot(scaled_low, returned, ((0,), (0,)))
    partial = partial.reshape(2, tok_dev, width)
    mine = lax.dynamic_index_in_dim(partial, core, 0, keepdims=False)
    theirs = lax.dynamic_index_in_dim(partial, 1 - core, 0, keepdims=False)
    student = (mine + swap(theirs)).astype(BF)
    pre_teacher = dot(teacher, teacher_rows)
    pre = pre_teacher + dot(student, student_rows)
    score = jnp.sum(gelu_tanh(pre) * critic_head[None, :], axis=1)
    dscore = -jax.nn.sigmoid(-score)
    dpre = (dscore[:, None] * critic_head[None, :] * gelu_slope(pre)).astype(BF)
    dpre2 = both(core, dpre, swap(dpre)).reshape(2 * tok_dev, -1)
    dstudent = dot(dpre2, student_rows, ((1,), (1,)))
    ds_high, ds_low = split(dstudent)
    grad_rows = dot(pick, ds_high) + dot(pick, ds_low)
    grad_out = (grad_rows * row_weight[:, None]).astype(BF)
    droute = lax.all_to_all(
        grad_out.reshape(chips, 2 * capacity, width), "yx", split_axis=0, concat_axis=0, tiled=True
    ).reshape(slots, width)

    parts = expert_backward(
        droute, inbound, hidden, coef_gate, coef_up, down_w, rows_in, 2 * capacity
    )
    total = lax.psum_scatter(
        parts.reshape(-1, width), "grp", scatter_dimension=0, tiled=True
    )
    grad_gate, grad_up, grad_down = unpack_grads(total, rows_in, half)
    return (grad_gate[None], grad_up[None], grad_down[None], score)


def solution(mesh):
    groups, members = mesh.devices.shape
    fine = Mesh(mesh.devices.reshape(groups, members // 2, 2), ("grp",) + EP)
    rows = P(("grp",) + EP, None)
    weights = P(EP, "grp", None)
    critic = P(EP, None)
    in_specs = (rows, rows, rows, rows, weights, weights, weights, critic, critic, P())
    out_specs = (weights, weights, weights, P(("grp",) + EP))
    return jax.shard_map(layer, mesh=fine, in_specs=in_specs, out_specs=out_specs, check_vma=False)
```

```python
import functools

import jax
import jax.numpy as jnp
from jax import lax
from jax.experimental import pallas as pl
from jax.experimental.pallas import tpu as pltpu
from jax.sharding import Mesh
from jax.sharding import PartitionSpec as P

TOP = 4
EP = ("yx", "c")
BF = jnp.bfloat16
F32 = jnp.float32


def gelu_tanh(value):
    inner = 0.7978845608 * (value + 0.044715 * value * value * value)
    return 0.5 * value * (1.0 + jnp.tanh(inner))


def gelu_slope(value):
    inner = 0.7978845608 * (value + 0.044715 * value * value * value)
    tangent = jnp.tanh(inner)
    return 0.5 * (1.0 + tangent) + 0.5 * value * (1.0 - tangent * tangent) * 0.7978845608 * (
        1.0 + 3.0 * 0.044715 * value * value
    )


def dot(left, right, dims=((1,), (0,))):
    return lax.dot_general(left, right, (dims, ((), ())), preferred_element_type=F32)


def split(value):
    high = value.astype(BF)
    return high, (value - high.astype(F32)).astype(BF)


def shift(value, axis, step):
    count = lax.axis_size(axis)
    return lax.ppermute(value, axis, [(i, (i + step) % count) for i in range(count)])


def swap(value):
    return shift(value, "c", 1)


def both(core, own, other):
    first = core == 0
    return jnp.stack([jnp.where(first, own, other), jnp.where(first, other, own)])


def ring_gather(block):
    count = lax.axis_size("grp")
    pieces = [block] + [None] * (count - 1)
    up = down = block
    for step in range(1, count // 2 + 1):
        up = shift(up, "grp", 1)
        pieces[step] = up
        if 2 * step < count:
            down = shift(down, "grp", -1)
            pieces[count - step] = down
    return pieces


def pair_up(value):
    count = lax.axis_size("grp")
    return lax.ppermute(value, "grp", [(i, i ^ 1) for i in range(count)])


def critic_half(side, shard):
    cols = shard.shape[1] // 2
    mine = lax.dynamic_slice_in_dim(shard, side * cols, cols, axis=1)
    return lax.all_gather(mine, EP, axis=0, tiled=True)


VMEM = pl.BlockSpec(memory_space=pltpu.VMEM)
SMEM = pl.BlockSpec(memory_space=pltpu.SMEM)
ANY = pl.BlockSpec(memory_space=pl.ANY)


def pack_kernel(gate_ref, up_ref, down_ref, out_ref):
    rows, hidden = gate_ref.shape
    half = hidden // 2
    out_ref[0:rows] = gate_ref[:, :half]
    out_ref[rows : 2 * rows] = gate_ref[:, half:]
    out_ref[2 * rows : 3 * rows] = up_ref[:, :half]
    out_ref[3 * rows : 4 * rows] = up_ref[:, half:]
    out_ref[4 * rows :] = down_ref[...]


def pack_weights(gate, up, down):
    rows = 4 * gate.shape[0] + down.shape[0]
    return pl.pallas_call(
        pack_kernel,
        out_shape=jax.ShapeDtypeStruct((rows, down.shape[1]), BF),
        in_specs=[VMEM] * 3,
        out_specs=VMEM,
        name="pack",
    )(gate, up, down)


def unpack_kernel(in_ref, gate_ref, up_ref, down_ref):
    rows, hidden = gate_ref.shape
    half = hidden // 2
    gate_ref[:, :half] = in_ref[0:rows].astype(F32)
    gate_ref[:, half:] = in_ref[rows : 2 * rows].astype(F32)
    up_ref[:, :half] = in_ref[2 * rows : 3 * rows].astype(F32)
    up_ref[:, half:] = in_ref[3 * rows : 4 * rows].astype(F32)
    down_ref[...] = in_ref[4 * rows :].astype(F32)


def unpack_grads(total, rows, half):
    return pl.pallas_call(
        unpack_kernel,
        out_shape=[
            jax.ShapeDtypeStruct((rows, 2 * half), F32),
            jax.ShapeDtypeStruct((rows, 2 * half), F32),
            jax.ShapeDtypeStruct((total.shape[0] - 4 * rows, total.shape[1]), F32),
        ],
        in_specs=[VMEM],
        out_specs=[VMEM] * 3,
        name="unpack",
    )(total)


def fetch(count, here_ref, pieces, target, sems, first):
    copies = []
    for k in range(count):
        at = lax.rem(here_ref[0] - k + count, count)
        piece = pieces[k].at[pl.ds(first, target.shape[1])]
        copies.append(pltpu.make_async_copy(piece, target.at[at], sems.at[k]))
    return copies


def forward_kernel(count, rows, chunk, here_ref, inbound_ref, *refs):
    pieces = refs[:count]
    hid_ref, coef_gate_ref, coef_up_ref, out_ref, down_ref, full, sems = refs[count:]

    @pl.when(pl.program_id(0) == 0)
    def _():
        copies = fetch(count, here_ref, pieces, full, sems, 0)
        for copy in copies:
            copy.start()
        for copy in copies:
            copy.wait()
        down_ref[...] = full[:, 4 * rows :]

    tile, width = out_ref.shape
    half = full.shape[2]
    routed = inbound_ref[:, :chunk].reshape(tile, width)
    out = jnp.zeros(out_ref.shape, F32)
    for part in range(2):
        gate_w = full[:, part * rows : (part + 1) * rows].reshape(width, half)
        up_w = full[:, (2 + part) * rows : (3 + part) * rows].reshape(width, half)
        gate = jnp.dot(routed, gate_w, preferred_element_type=F32)
        up = jnp.dot(routed, up_w, preferred_element_type=F32)
        sig = jax.nn.sigmoid(gate)
        silu = gate * sig
        hid = (silu * up).astype(BF)
        span = slice(part * half, (part + 1) * half)
        hid_ref[:, span] = hid
        coef_up_ref[:, span] = silu.astype(BF)
        coef_gate_ref[:, span] = (up * (sig + silu * (1.0 - sig))).astype(BF)
        group = count // 2
        down_w = full[part * group : (part + 1) * group, 4 * rows :].reshape(half, width)
        out += jnp.dot(hid, down_w, preferred_element_type=F32)
    out_ref[...] = out.astype(BF)


def expert_forward(here, inbound, pieces, rows, chunk, steps=2):
    count = len(pieces)
    chips, taken, width = inbound.shape
    slots = chips * chunk
    tile = slots // steps
    high, half = pieces[0].shape
    down = (count, high - 4 * rows, half)
    hidden = 2 * half
    block = lambda cols: pl.BlockSpec((tile, cols), lambda i: (i, 0))
    wide = jax.ShapeDtypeStruct((slots, hidden), BF)
    return pl.pallas_call(
        functools.partial(forward_kernel, count, rows, chunk),
        grid=(steps,),
        out_shape=[
            wide,
            wide,
            wide,
            jax.ShapeDtypeStruct((slots, width), BF),
            jax.ShapeDtypeStruct(down, BF),
        ],
        in_specs=[SMEM, pl.BlockSpec((chips // steps, taken, width), lambda i: (i, 0, 0))]
        + [ANY] * count,
        out_specs=[
            block(hidden),
            block(hidden),
            block(hidden),
            block(width),
            pl.BlockSpec(down, lambda i: (0, 0, 0)),
        ],
        scratch_shapes=[
            pltpu.VMEM((count,) + pieces[0].shape, BF),
            pltpu.SemaphoreType.DMA((count,)),
        ],
        cost_estimate=pl.CostEstimate(
            flops=6 * slots * width * hidden,
            transcendentals=slots * hidden,
            bytes_accessed=6 * slots * hidden + 6 * width * hidden,
        ),
        name="expert_forward",
    )(here, inbound, *pieces)


def backward_kernel(
    rows, chunk, droute_ref, inbound_ref, hid_ref, cg_ref, cu_ref, down, out_ref, parts, out_sems
):
    step = pl.program_id(0)
    slots, width = droute_ref.shape
    half = hid_ref.shape[1]
    count = out_ref.shape[0]
    each = down.shape[1]
    take = count // 2
    droute = droute_ref[...]
    routed = inbound_ref[:, :chunk].reshape(slots, width)
    down_w = down[...].reshape(half, width)
    dhid = lax.dot_general(droute, down_w, (((1,), (1,)), ((), ())), preferred_element_type=F32)
    dgate = (dhid * cg_ref[...].astype(F32)).astype(BF)
    dup = (dhid * cu_ref[...].astype(F32)).astype(BF)
    rows_dot = functools.partial(
        lax.dot_general, dimension_numbers=(((0,), (0,)), ((), ())), preferred_element_type=F32
    )
    part_down = rows_dot(hid_ref[...], droute).astype(BF).reshape(take, each, width)
    part_gate = rows_dot(routed, dgate).astype(BF).reshape(count, rows, half)
    part_up = rows_dot(routed, dup).astype(BF).reshape(count, rows, half)

    def leaving(at):
        places = [(pl.ds(at * take, take), pl.ds(4 * rows, each))]
        places += [(slice(None), pl.ds(block * rows, rows)) for block in (at, 2 + at)]
        return [
            pltpu.make_async_copy(parts.at[place], out_ref.at[place], out_sems.at[3 * at + k])
            for k, place in enumerate(places)
        ]

    for at in range(2):

        @pl.when(step == at)
        def _():
            parts[at * take : (at + 1) * take, 4 * rows :] = part_down
            parts[:, at * rows : (at + 1) * rows] = part_gate
            parts[:, (2 + at) * rows : (3 + at) * rows] = part_up
            for copy in leaving(at):
                copy.start()

    @pl.when(step == 1)
    def _():
        for at in range(2):
            for copy in leaving(at):
                copy.wait()


def expert_backward(droute, inbound, hid, coef_gate, coef_up, down, rows, chunk):
    slots, width = droute.shape
    hidden = hid.shape[1]
    block = pl.BlockSpec((slots, hidden // 2), lambda i: (0, i))
    count, each = down.shape[:2]
    shape = (count, 4 * rows + each, width)
    return pl.pallas_call(
        functools.partial(backward_kernel, rows, chunk),
        grid=(2,),
        out_shape=jax.ShapeDtypeStruct(shape, BF),
        in_specs=[
            pl.BlockSpec((slots, width), lambda i: (0, 0)),
            pl.BlockSpec(inbound.shape, lambda i: (0, 0, 0)),
            block,
            block,
            block,
            pl.BlockSpec((count // 2, each, width), lambda i: (i, 0, 0)),
        ],
        out_specs=ANY,
        scratch_shapes=[
            pltpu.VMEM(shape, BF),
            pltpu.SemaphoreType.DMA((6,)),
        ],
        cost_estimate=pl.CostEstimate(
            flops=8 * slots * width * hidden,
            transcendentals=0,
            bytes_accessed=6 * slots * hidden + 6 * width * hidden,
        ),
        name="expert_backward",
    )(droute, inbound, hid, coef_gate, coef_up, down)


def layer(
    tokens,
    teacher,
    expert_ids,
    route_weights,
    w_gate,
    w_up,
    w_down,
    critic_teacher,
    critic_student,
    critic_head,
):
    core = lax.axis_index("c")
    chips = lax.axis_size("yx")
    experts = 2 * chips
    tok_dev, width = tokens.shape
    capacity = 3 * tok_dev * TOP // (2 * experts)
    slots = experts * capacity
    hidden_all = w_gate.shape[2]
    half = hidden_all // 2
    rows_in = w_gate.shape[1]

    side = lax.axis_index("grp") % 2
    teacher_rows = critic_half(side, critic_teacher)
    here = lax.axis_index("grp").astype(jnp.int32).reshape(1)
    pieces = ring_gather(pack_weights(w_gate[0], w_up[0], w_down[0]))

    other_teacher = pair_up(teacher)

    meta = jnp.concatenate([expert_ids.T.astype(F32), route_weights.T])
    tok2 = both(core, tokens, swap(tokens)).reshape(2 * tok_dev, width)
    meta2 = both(core, meta, swap(meta))
    ids = meta2[:, :TOP].astype(jnp.int32)
    weights = meta2[:, TOP:]
    member = ids[:, :, None, :] == jnp.arange(experts, dtype=jnp.int32)[None, None, :, None]
    count = jnp.sum(member.astype(F32), axis=1).astype(BF)
    order = jnp.arange(tok_dev)
    earlier = (order[:, None] < order[None, :]).astype(BF)
    before = lax.dot_general(count, earlier, (((2,), (0,)), ((), ())), preferred_element_type=F32)
    rank = jnp.sum(jnp.where(member, before[:, None], 0.0), axis=2).astype(jnp.int32)
    source = jnp.arange(2, dtype=jnp.int32)[:, None, None]
    place = (ids // 2) * (2 * capacity) + source * capacity + rank
    place = jnp.where(ids % 2 == core, place, -1)
    place = place.transpose(1, 0, 2).reshape(TOP, 2 * tok_dev)
    weights = weights.transpose(1, 0, 2).reshape(TOP, 2 * tok_dev)
    hits = place[:, None, :] == jnp.arange(slots, dtype=jnp.int32)[None, :, None]
    pick = jnp.sum(hits.astype(F32), axis=0).astype(BF)
    scaled = jnp.sum(jnp.where(hits, weights[:, None, :], 0.0), axis=0)
    row_weight = jnp.sum(scaled, axis=1)
    scaled_high, scaled_low = split(scaled)

    outbound = dot(pick, tok2).astype(BF).reshape(chips, 2 * capacity, width)
    rows_st = critic_student.shape[0]
    outbound = jnp.concatenate(
        [outbound, jnp.broadcast_to(critic_student[None], (chips, rows_st, width))], axis=1
    )
    inbound = lax.all_to_all(outbound, "yx", split_axis=0, concat_axis=0, tiled=True)
    student_half = inbound[:, 2 * capacity :]
    student_other = swap(student_half)
    student_rows = (
        both(core, student_half, student_other).transpose(1, 0, 2, 3).reshape(width, -1)
    )

    hidden, coef_gate, coef_up, expert_out, down_w = expert_forward(
        here, inbound, pieces, rows_in, 2 * capacity
    )
    returned = lax.all_to_all(
        expert_out.reshape(chips, 2 * capacity, width),
        "yx",
        split_axis=0,
        concat_axis=0,
        tiled=True,
    ).reshape(slots, width)

    partial = dot(scaled_high, returned, ((0,), (0,))) + dot(scaled_low, returned, ((0,), (0,)))
    partial = partial.reshape(2, tok_dev, width)
    mine = lax.dynamic_index_in_dim(partial, core, 0, keepdims=False)
    theirs = lax.dynamic_index_in_dim(partial, 1 - core, 0, keepdims=False)
    student = (mine + swap(theirs)).astype(BF)
    own_pre = dot(teacher, teacher_rows)
    other_pre = dot(other_teacher, teacher_rows)
    own_pre, other_pre = lax.optimization_barrier((own_pre, other_pre))
    got_pre = pair_up(other_pre)
    even = side == 0
    pre_teacher = jnp.concatenate(
        [jnp.where(even, own_pre, got_pre), jnp.where(even, got_pre, own_pre)], axis=1
    )
    pre = pre_teacher + dot(student, student_rows)
    score = jnp.sum(gelu_tanh(pre) * critic_head[None, :], axis=1)
    dscore = -jax.nn.sigmoid(-score)
    dpre = (dscore[:, None] * critic_head[None, :] * gelu_slope(pre)).astype(BF)
    dpre2 = both(core, dpre, swap(dpre)).reshape(2 * tok_dev, -1)
    dstudent = dot(dpre2, student_rows, ((1,), (1,)))
    ds_high, ds_low = split(dstudent)
    grad_rows = dot(pick, ds_high) + dot(pick, ds_low)
    grad_out = (grad_rows * row_weight[:, None]).astype(BF)
    droute = lax.all_to_all(
        grad_out.reshape(chips, 2 * capacity, width), "yx", split_axis=0, concat_axis=0, tiled=True
    ).reshape(slots, width)

    parts = expert_backward(
        droute, inbound, hidden, coef_gate, coef_up, down_w, rows_in, 2 * capacity
    )
    total = lax.psum_scatter(
        parts.reshape(-1, width), "grp", scatter_dimension=0, tiled=True
    )
    grad_gate, grad_up, grad_down = unpack_grads(total, rows_in, half)
    return (grad_gate[None], grad_up[None], grad_down[None], score)


def solution(mesh):
    groups, members = mesh.devices.shape
    fine = Mesh(mesh.devices.reshape(groups, members // 2, 2), ("grp",) + EP)
    rows = P(("grp",) + EP, None)
    weights = P(EP, "grp", None)
    critic = P(EP, None)
    in_specs = (rows, rows, rows, rows, weights, weights, weights, critic, critic, P())
    out_specs = (weights, weights, weights, P(("grp",) + EP))
    return jax.shard_map(layer, mesh=fine, in_specs=in_specs, out_specs=out_specs, check_vma=False)
```
